256 devices in a mesh: blk: 16 (over z_lo, x), rep: 16 (over z_hi, y, core).
Axes of the slice: x: 4, y: 4, z: 8 (z_hi: 2, z_lo: 4; z = z_hi * 4 + z_lo), core: 2. Of those that a mesh axis runs over, the one named last changes fastest.
Arguments:
- features: bfloat16 [65536, 128], P('blk'), may hold values from -6 to 6
- weight: bfloat16 [128, 256], replicated, may hold values from -0.5 to 0.5
- bias: float32 [256], replicated, may hold values from -3 to 3
- tile_values: bfloat16 [16, 16, 160, 128, 128], P('blk', 'rep'), may hold values from 0 to 0.029541016
- tile_place: int32 [16, 16, 160], P('blk', 'rep'), may hold values from 0 to 1023, as said below
- tile_count: int32 [16, 16], P('blk', 'rep'), may hold values from 1 to 160, as said below
Outputs:
- activations: bfloat16 [65536, 256], P('blk')
The draws below stay inside these ranges and needn't reach their ends.
Inputs may be any that keep to these rules, and one draw needn't show every extreme that they name: `tile_place`: within one pair of destination block and section the 160 positions are distinct. `tile_count`: some pair of destination block and section has all 160 slots occupied.
All inputs are finite; a program needn't handle non-finite values.
Results may differ from the reference program's by a relative error of at most 0.0046.
Values may be sent and summed in bfloat16 or wider, within the bound.
No kernel may reach another device: no remote copies, remote signals or barrier semaphores. Data moves between devices by JAX's collectives and lax.ppermute only.
A program may use at most 128 MiB of HBM per device.

```python
import jax
import jax.numpy as jnp
from jax import lax

F_IN = 128
HIDDEN_SIZE = 256
TILE = 128
ROWS_BLK = 4096
SLOTS = 160
BLOCKS = 16
NODES = 65536


def draw_tile_count(key, part):
    base = jax.random.fold_in(key, 11)
    first_key, second_key, third_key = jax.random.split(base, 3)
    first_draw = jax.random.randint(first_key, (BLOCKS * BLOCKS,), 1, SLOTS + 1)
    second_draw = jax.random.randint(second_key, (BLOCKS * BLOCKS,), 1, SLOTS + 1)
    counts = jnp.minimum(first_draw, second_draw)
    chosen = jax.random.randint(third_key, (), 0, BLOCKS * BLOCKS)
    counts = jnp.where(jnp.arange(BLOCKS * BLOCKS, dtype=jnp.int32) == chosen, SLOTS, counts)
    return counts.reshape(BLOCKS, BLOCKS).astype(jnp.int32)


def draw_tile_place(key, part):
    base = jax.random.fold_in(key, 23)
    positions = ROWS_BLK // TILE * (ROWS_BLK // TILE)
    scores = jax.random.randint(base, (BLOCKS, BLOCKS, positions), 0, 2 ** 30 // positions)
    scores = scores * positions + jnp.arange(positions, dtype=jnp.int32)
    order = jnp.argsort(scores, axis=-1)
    return order[:, :, :SLOTS].astype(jnp.int32)


def block_scale(key, extent, shards, smallest, top_value):
    def one(dim, blocks):
        steps = jax.random.uniform(jax.random.fold_in(jax.random.fold_in(key, 6), dim), (blocks,), jnp.float32, smallest / len(shards), top_value / len(shards))
        return jnp.repeat(jnp.exp(steps), extent[dim] // blocks).reshape((-1,) + (1,) * (len(extent) - dim - 1))

    level = one(*shards[0])
    for cut in shards[1:]:
        level = level * one(*cut)
    return level


def centred(key, shape, spread, most, shards=(), kind=jnp.bfloat16):
    gain = block_scale(key, shape, shards, -0.22, 0.18) if shards else 1.0
    values = jax.random.normal(key, shape, jnp.float32) * spread * gain
    return jnp.minimum(jnp.maximum(values, -most), most).astype(kind)


def setup_inputs(seed: int = 0) -> dict:
    arg_keys = jax.random.split(jax.random.key(seed), 7)
    return {
        "features": centred(arg_keys[0], (NODES, F_IN), 1.0, 6.0, ((0, 16),)),
        "weight": centred(arg_keys[1], (F_IN, HIDDEN_SIZE), F_IN ** -0.5, 0.5),
        "bias": centred(arg_keys[2], (HIDDEN_SIZE,), 0.5, 3.0, (), jnp.float32),
        "tile_values": jnp.clip(0.029541016 * jax.random.uniform(arg_keys[3], (BLOCKS, BLOCKS, SLOTS, TILE, TILE), jnp.float32) ** block_scale(arg_keys[3], (BLOCKS, BLOCKS, SLOTS, TILE, TILE), ((0, 16), (1, 16)), -0.2, 0.2), 0.0, 0.029541016).astype(jnp.bfloat16),
        "tile_place": draw_tile_place(jax.random.fold_in(arg_keys[6], 71), 0),
        "tile_count": draw_tile_count(jax.random.fold_in(arg_keys[6], 71), 0),
    }


def reference(features, weight, bias, tile_values, tile_place, tile_count):
    row_tiles = ROWS_BLK // TILE
    blocked = features.reshape(BLOCKS, row_tiles, TILE, F_IN)
    section_ids = jnp.arange(BLOCKS, dtype=jnp.int32)
    slot_ids = jnp.arange(SLOTS, dtype=jnp.int32)
    tile_rows = jnp.arange(row_tiles, dtype=jnp.int32)

    def one_block(dest):
        sources = ((dest - section_ids) % BLOCKS).astype(jnp.int32)
        place = tile_place[dest]
        column = place % row_tiles
        target = place // row_tiles
        pieces = blocked[sources[:, None], column]
        products = jnp.einsum("skij,skjf->skif", tile_values[dest].astype(jnp.float32), pieces.astype(jnp.float32))
        live = (slot_ids[None, :] < tile_count[dest][:, None]).astype(jnp.float32)
        picker = (target[:, :, None] == tile_rows[None, None, :]).astype(jnp.float32) * live[:, :, None]
        summed = jnp.einsum("skr,skif->rif", picker, products, precision=lax.Precision.HIGHEST)
        return summed.reshape(ROWS_BLK, F_IN)

    summed = lax.map(one_block, jnp.arange(BLOCKS, dtype=jnp.int32)).reshape(NODES, F_IN)
    aggregated = summed.astype(jnp.bfloat16)
    output = jnp.dot(aggregated, weight, preferred_element_type=jnp.float32) + bias
    return jnp.maximum(output, 0.0).astype(jnp.bfloat16)
```

```python
import functools

import jax
import jax.numpy as jnp
from jax import lax
from jax.experimental import pallas as pl
from jax.experimental.pallas import tpu as pltpu
from jax.sharding import Mesh
from jax.sharding import PartitionSpec as P

TILE = 128
ROW_TILES = 32
HALF_TILES = 16
SLOTS = 160
UNROLL = 4
AXES = ("blk", "zh", "y", "core")
LIST = 128
VMEM = pltpu.MemorySpace.VMEM

SOURCES = (
    (
        "cb56a8fe092d3417", "231fd58bc9a7460e", "3b2075ea19c6d48f", "30546bea81d27cf9",
        "07415362deb8caf9", "46513072c9edbaf8", "5673429018facbde", "31264d570baf8c9e",
        "6ca8725103b4fde9", "623570491efb8acd", "045631ea72fd8bc9", "60247315cfade98b",
        "7053de8a2164bc9f", "7263da90415fecb8", "71e40952638dfbca", "7ed9f2534b016ac8",
    ),
    (
        "3f78e9cb0d5a4126", "135b79ed8fa4206c", "0afb429de56173c8", "56423fdc9107eba8",
        "07243651abd9efc8", "013524769eb8cdfa", "4025619c378daefb", "054637812ae9dbfc",
        "03ea4571d6c2bf89", "6023147f598deacb", "326574df10a8ec9b", "052374861fb9eacd",
        "7612adbc0543f8e9", "574ba0936128fdce", "46b93c1f0758d2ae", "5a8ec2670134db9f",
    ),
    (
        "8043dabc6fe97251", "712a6b8ecdf30549", "175462e8af0bd39c", "63017d8ab254ce9f",
        "53762401fe8cadb9", "734152608eabd9cf", "273156ae40c9fd8b", "403127ef68db9c5a",
        "49362170f85edacb", "4052317d69bafc8e", "60134275a8e9dbcf", "71205436e98bcfad",
        "153798de4062bcfa", "2054edf7316ba89c", "35c09d6241a7bfe8", "39abd01764285cef",
    ),
    (
        "1edafc982b754063", "1754dce98bf0632a", "71063dce98f254ba", "16304f89e72b5cda",
        "503216748facb9de", "26037514bcdf8ea9", "12463570b8fa9cde", "631572b048edca9f",
        "f0c43625718a9bde", "1640537ba2c8def9", "012463875fcdb9ea", "04752631b9a8dcef",
        "5042eaf96731db8c", "1208df65437cea9b", "627b5a0931e4fc8d", "08cbf451267a3ed9",
    ),
)


def feature_routes(chunk):
    pairs = []
    for block in range(16):
        for section in range(16):
            replica = int(SOURCES[chunk][block][section], 16)
            target = (block + section) % 16
            pairs.append((block * 16 + replica, target * 16 + section))
    return pairs


def device_pairs(step):
    pairs = []
    for index in range(256):
        blk, rest = divmod(index, 16)
        zh, rest = divmod(rest, 8)
        y, core = divmod(rest, 2)
        zh, y, core = step(zh, y, core)
        pairs.append((index, blk * 16 + zh * 8 + y * 2 + core))
    return pairs


def moved(value, pairs):
    return lax.ppermute(value, AXES, pairs)


def prepare_kernel(place, count, slot_of, column_of, row_of, pairs, position):
    total = count[0]

    @pl.loop(0, ROW_TILES)
    def _(i):
        position[i] = 0

    @pl.loop(0, total)
    def _(k):
        i = place[k] >> 5
        position[i] = position[i] + 1

    @pl.loop(0, 4 * LIST)
    def _(q):
        slot_of[q] = 0
        column_of[q] = ROW_TILES

    @pl.loop(0, 2 * LIST)
    def _(q):
        row_of[q] = 0

    for half in range(2):

        def lay(i, start):
            number = (position[i] + 1) >> 1
            position[i] = 2 * start

            def mark(q, carry):
                row_of[q] = i - half * HALF_TILES
                return carry

            lax.fori_loop(start, start + number, mark, 0)
            return start + number

        first = half * LIST
        end = lax.fori_loop(half * HALF_TILES, (half + 1) * HALF_TILES, lay, first)
        pairs[half] = end - first

    @pl.loop(0, total)
    def _(k):
        p = place[k]
        i = p >> 5
        q = position[i]
        position[i] = q + 1
        slot_of[q] = k
        column_of[q] = p & (ROW_TILES - 1)


def prepared(place, count):
    smem = pl.BlockSpec(memory_space=pltpu.SMEM)
    return pl.pallas_call(
        prepare_kernel,
        out_shape=(
            jax.ShapeDtypeStruct((4 * LIST,), jnp.int32),
            jax.ShapeDtypeStruct((4 * LIST,), jnp.int32),
            jax.ShapeDtypeStruct((2 * LIST,), jnp.int32),
            jax.ShapeDtypeStruct((2,), jnp.int32),
        ),
        in_specs=[smem, smem],
        out_specs=(smem, smem, smem, smem),
        scratch_shapes=[pltpu.SMEM((ROW_TILES,), jnp.int32)],
        cost_estimate=pl.CostEstimate(flops=0, bytes_accessed=16_000_000, transcendentals=0),
        compiler_params=pltpu.CompilerParams(vmem_limit_bytes=1 << 20),
        name="prepare",
    )(place, count)


def product_kernel(half, slot_of, column_of, row_of, pairs, held, source, out):
    h = half[0]
    base = h * LIST
    out[...] = jnp.zeros_like(out)
    steps = (pairs[h] + UNROLL - 1) // UNROLL

    @pl.loop(0, steps)
    def _(step):
        first = base + step * UNROLL
        terms = []
        for u in range(UNROLL):
            q = 2 * (first + u)
            left = jnp.concatenate([held[slot_of[q]], held[slot_of[q + 1]]], axis=1)
            right = jnp.concatenate([source[column_of[q]], source[column_of[q + 1]]], axis=0)
            terms.append(jnp.dot(left, right, preferred_element_type=jnp.float32))
        for u in range(UNROLL):
            row = row_of[first + u]
            out[row] = out[row] + terms[u]


def half_product(half, lists, held, source):
    smem = pl.BlockSpec(memory_space=pltpu.SMEM)
    vmem = pl.BlockSpec(memory_space=pltpu.VMEM)
    return pl.pallas_call(
        product_kernel,
        out_shape=jax.ShapeDtypeStruct((HALF_TILES, TILE, TILE), jnp.float32),
        in_specs=[smem] * 5 + [vmem] * 2,
        out_specs=vmem,
        cost_estimate=pl.CostEstimate(flops=400_000_000, bytes_accessed=9_000_000, transcendentals=0),
        compiler_params=pltpu.CompilerParams(vmem_limit_bytes=24 << 20),
        name="products",
    )(half, *lists, held, source)


def shards(features, weight, bias, tile_values, tile_place, tile_count):
    y = lax.axis_index("y")
    core = lax.axis_index("core")
    chunks = len(SOURCES)
    rows = features.shape[0] // chunks
    parts = [
        moved(features[n * rows : (n + 1) * rows], feature_routes(n)) for n in range(chunks)
    ]
    lists = prepared(tile_place[0, 0], tile_count[0])
    held = tile_values[0, 0]
    parts.append(jnp.zeros((TILE, features.shape[1]), features.dtype))
    source = jnp.concatenate(parts, axis=0).reshape(ROW_TILES + 1, TILE, features.shape[1])

    other_core = device_pairs(lambda zh, y, core: (zh, y, 1 - core))
    other_half = device_pairs(lambda zh, y, core: (1 - zh, y, core))
    up = device_pairs(lambda zh, y, core: (zh, (y + 1) % 4, core))
    down = device_pairs(lambda zh, y, core: (zh, (y - 1) % 4, core))
    across = device_pairs(lambda zh, y, core: (zh, (y + 2) % 4, core))

    given = half_product((1 - core).reshape(1), lists, held, source)
    arrived = moved(given, other_core)
    kept = half_product(core.reshape(1), lists, held, source)

    def quarter(step):
        at = ((y + step) % 4) * 4
        size = 4
        part = lax.dynamic_slice_in_dim(kept, at, size) + lax.dynamic_slice_in_dim(arrived, at, size)
        return part.reshape(size * TILE, TILE)

    with jax.named_scope("scatter_y"):
        sums = [
            moved(quarter(step).astype(jnp.bfloat16), pairs)
            for step, pairs in ((1, up), (3, down), (2, across))
        ]
        mine = quarter(0)
        for part in sums:
            mine = mine + part.astype(jnp.float32)
    with jax.named_scope("pair_z"):
        sent = mine.astype(jnp.bfloat16)
        back = moved(sent, other_half)
        aggregated = (sent.astype(jnp.float32) + back.astype(jnp.float32)).astype(jnp.bfloat16)
    with jax.named_scope("gather_y"):
        near = [aggregated] + [moved(aggregated, pairs) for pairs in (down, across, up)]
    with jax.named_scope("gather_core"):
        far = [moved(part, other_core) for part in near]
    return finished(near, far, weight, bias, y, core)


def finish_kernel(where, *refs):
    parts, (weight, bias, out, stage, sem) = refs[:8], refs[8:]
    y, core = where[0], where[1]
    rows = parts[0].shape[0]
    copies = []
    for n in range(8):
        slot = n % 4
        if n >= 4:
            copies[n - 4].wait()
        half = core if n < 4 else 1 - core
        quarter = (y + n) & 3
        result = jnp.dot(parts[n][...], weight[...], preferred_element_type=jnp.float32) + bias[...]
        stage[slot] = jnp.maximum(result, 0.0).astype(stage.dtype)
        start = pl.multiple_of((half * 4 + quarter) * rows, rows)
        copy = pltpu.make_async_copy(stage.at[slot], out.at[pl.ds(start, rows)], sem.at[slot])
        copy.start()
        copies.append(copy)
    for copy in copies[4:]:
        copy.wait()


def finished(near, far, weight, bias, y, core):
    vmem = pl.BlockSpec(memory_space=pltpu.VMEM)
    rows = near[0].shape[0]
    hidden = weight.shape[1]
    return pl.pallas_call(
        finish_kernel,
        out_shape=jax.ShapeDtypeStruct((8 * rows, hidden), jnp.bfloat16),
        in_specs=[pl.BlockSpec(memory_space=pltpu.SMEM)] + [vmem] * 10,
        out_specs=pl.BlockSpec(memory_space=pl.ANY),
        scratch_shapes=[
            pltpu.VMEM((4, rows, hidden), jnp.bfloat16),
            pltpu.SemaphoreType.DMA((4,)),
        ],
        compiler_params=pltpu.CompilerParams(vmem_limit_bytes=24 << 20),
        name="finish",
    )(jnp.stack([y, core]), *near, *far, weight, bias.reshape(1, hidden))


def solution(mesh):
    split = Mesh(mesh.devices.reshape(16, 2, 4, 2), AXES)
    rep = AXES[1:]
    in_specs = (
        P("blk", None),
        P(),
        P(),
        P("blk", rep, None, None, None),
        P("blk", rep, None),
        P("blk", rep),
    )
    return jax.shard_map(
        shards, mesh=split, in_specs=in_specs, out_specs=P("blk", None), check_vma=False
    )
```

```python
import functools

import jax
import jax.numpy as jnp
from jax import lax
from jax.experimental import pallas as pl
from jax.experimental.pallas import tpu as pltpu
from jax.sharding import Mesh
from jax.sharding import PartitionSpec as P

TILE = 128
ROW_TILES = 32
HALF_TILES = 16
SLOTS = 160
UNROLL = 4
AXES = ("blk", "zh", "y", "core")
LIST = 128
VMEM = pltpu.MemorySpace.VMEM

SOURCES = (
    (
        0x10734ad70e2a6514, 0x7250136f88c2451d, 0x012413dfdb0475fe, 0x06227acef1056d8f,
        0x10142740aef98ea8, 0x0524116ca92b89fe, 0x61206497adb9fcae, 0x0120428c89cbefdd,
        0x41204327f56cbc9f, 0x012344767fb88bdf, 0x12056430b2bc8fcf, 0x16424d357ea8dfbc,
        0x1150baec4062dcff, 0x0144daf236a9eef8, 0x13fcae632698bdf9, 0x08abf35129cbdacf,
    ),
    (
        0x214357f969c05263, 0x300c47481cb5627f, 0x6317578af962028c, 0x101554e987234bfd,
        0x05231356d8bccb9e, 0x1002536eecf8dadf, 0x151446f2e8cbd89e, 0x16734a6fbeb8dc9e,
        0x31530561a0c29ae9, 0x36507021351cec9a, 0x314317570ea9cdbd, 0x751127f008caec9e,
        0x0735d4e81635ab8d, 0x062bed97705cdb8c, 0x30a98c5150ebdfae, 0x08d9b56f1ae85cd9,
    ),
)
EXTRA = (
    (
        0xc026, 0x4904, 0x058a, 0x0506, 0x13c1, 0x0214, 0x4050, 0x40c5,
        0x8841, 0x1650, 0x8b04, 0x0030, 0x6201, 0x1444, 0xc280, 0x2c10,
    ),
    (
        0x0199, 0x003a, 0x0861, 0x0029, 0x0c0a, 0x1482, 0x0309, 0x0302,
        0x111e, 0x088d, 0x2023, 0x1485, 0x009c, 0x08a9, 0x0446, 0x002e,
    ),
)


def feature_routes():
    routes = ([], [], [])
    sent, taken = [0] * 256, [0] * 256
    for chunk in range(2):
        for block in range(16):
            for section in range(16):
                replica = SOURCES[chunk][block] >> (4 * (15 - section)) & 15
                source = block * 16 + replica
                target = (block + section) % 16 * 16 + section
                if EXTRA[chunk][block] >> section & 1:
                    routes[2].append((source, target))
                    sent[source] = chunk
                    taken[target] = 1 + chunk
                else:
                    routes[chunk].append((source, target))
    return routes, sent, taken


def device_pairs(step):
    pairs = []
    for index in range(256):
        blk, rest = divmod(index, 16)
        zh, rest = divmod(rest, 8)
        y, core = divmod(rest, 2)
        zh, y, core = step(zh, y, core)
        pairs.append((index, blk * 16 + zh * 8 + y * 2 + core))
    return pairs


def moved(value, pairs):
    return lax.ppermute(value, AXES, pairs)


def prepare_kernel(place, count, tiles, held, slot_of, column_of, row_of, pairs, position, sem):
    total = count[0]
    fetch = pltpu.make_async_copy(tiles, held, sem)
    fetch.start()

    for i in range(ROW_TILES + 1):
        position[i] = 0

    def number(k, carry):
        i = jnp.where(k < total, place[k] >> 5, ROW_TILES)
        position[i] = position[i] + 1
        return carry

    lax.fori_loop(0, SLOTS, number, 0, unroll=8)

    for half in range(2):
        first = half * LIST
        start = first
        for i in range(half * HALF_TILES, (half + 1) * HALF_TILES):
            n = position[i]
            position[i] = 2 * start
            start = start + ((n + 1) >> 1)
            last = jnp.where((n & 1) == 1, 2 * start - 1, 4 * LIST)
            slot_of[last] = 0
            column_of[last] = ROW_TILES
        pairs[half] = start - first
        for u in range(UNROLL - 1):
            row_of[start + u] = 0
            for v in range(2):
                slot_of[2 * (start + u) + v] = 0
                column_of[2 * (start + u) + v] = ROW_TILES
    position[ROW_TILES] = 4 * LIST + 8

    def lay(k, carry):
        p = place[k]
        i = jnp.where(k < total, p >> 5, ROW_TILES)
        q = position[i]
        position[i] = q + jnp.where(k < total, 1, 0)
        slot_of[q] = k
        column_of[q] = p & (ROW_TILES - 1)
        row_of[q >> 1] = i & (HALF_TILES - 1)
        return carry

    lax.fori_loop(0, SLOTS, lay, 0, unroll=8)
    fetch.wait()


def prepared(tiles, place, count):
    smem = pl.BlockSpec(memory_space=pltpu.SMEM)
    return pl.pallas_call(
        prepare_kernel,
        out_shape=(
            pltpu.VMEM((SLOTS, TILE, TILE), tiles.dtype),
            jax.ShapeDtypeStruct((4 * LIST + 128,), jnp.int32),
            jax.ShapeDtypeStruct((4 * LIST + 128,), jnp.int32),
            jax.ShapeDtypeStruct((2 * LIST + 128,), jnp.int32),
            jax.ShapeDtypeStruct((2,), jnp.int32),
        ),
        in_specs=[smem, smem, pl.BlockSpec(memory_space=pl.ANY)],
        out_specs=(pl.BlockSpec(memory_space=pltpu.VMEM), smem, smem, smem, smem),
        scratch_shapes=[pltpu.SMEM((ROW_TILES + 1,), jnp.int32), pltpu.SemaphoreType.DMA],
        cost_estimate=pl.CostEstimate(flops=0, bytes_accessed=16_000_000, transcendentals=0),
        compiler_params=pltpu.CompilerParams(vmem_limit_bytes=1 << 20),
        name="prepare",
    )(place, count, tiles)


def product_kernel(choice, slot_of, column_of, row_of, pairs, held, first, second, extra, given, kept, source):
    core, taken = choice[0], choice[1]
    rows = HALF_TILES

    for chunk, plain in enumerate((first, second)):
        place = pl.ds(chunk * rows, rows)

        @pl.when(taken == 1 + chunk)
        def _():
            source[place] = extra[...]

        @pl.when(taken != 1 + chunk)
        def _():
            source[place] = plain[...]

    source[ROW_TILES] = jnp.zeros((TILE, TILE), source.dtype)

    for half, out in ((1 - core, given), (core, kept)):
        out[...] = jnp.zeros_like(out)
        base = half * LIST
        steps = (pairs[half] + UNROLL - 1) // UNROLL

        @pl.loop(0, steps)
        def _(step):
            start = base + step * UNROLL
            terms = []
            for u in range(UNROLL):
                q = 2 * (start + u)
                left = jnp.concatenate([held[slot_of[q]], held[slot_of[q + 1]]], axis=1)
                right = jnp.concatenate([source[column_of[q]], source[column_of[q + 1]]], axis=0)
                terms.append(jnp.dot(left, right, preferred_element_type=jnp.float32))
            for u in range(UNROLL):
                row = row_of[start + u]
                out[row] = out[row] + terms[u]


def products(choice, lists, held, parts):
    smem = pl.BlockSpec(memory_space=pltpu.SMEM)
    vmem = pl.BlockSpec(memory_space=pltpu.VMEM)
    half = jax.ShapeDtypeStruct((HALF_TILES, TILE, TILE), jnp.float32)
    tiles = [part.reshape(HALF_TILES, TILE, TILE) for part in parts]
    return pl.pallas_call(
        product_kernel,
        out_shape=(half, half),
        in_specs=[smem] * 5 + [vmem] * 4,
        out_specs=(vmem, vmem),
        scratch_shapes=[pltpu.VMEM((ROW_TILES + 1, TILE, TILE), parts[0].dtype)],
        cost_estimate=pl.CostEstimate(flops=800_000_000, bytes_accessed=9_000_000, transcendentals=0),
        compiler_params=pltpu.CompilerParams(vmem_limit_bytes=8 << 20),
        name="products",
    )(choice, *lists, held, *tiles)


def shards(features, weight, bias, tile_values, tile_place, tile_count):
    y = lax.axis_index("y")
    core = lax.axis_index("core")
    routes, sent, taken = feature_routes()
    me = lax.axis_index(AXES)
    rows = features.shape[0] // 2
    pieces = [features[:rows], features[rows:]]
    pieces.append(lax.dynamic_slice_in_dim(features, jnp.asarray(sent, jnp.int32)[me] * rows, rows))
    parts = [moved(piece, route) for piece, route in zip(pieces, routes)]
    held, *lists = prepared(tile_values[0, 0], tile_place[0, 0], tile_count[0])
    choice = jnp.stack([core, jnp.asarray(taken, jnp.int32)[me]])

    other_core = device_pairs(lambda zh, y, core: (zh, y, 1 - core))
    other_half = device_pairs(lambda zh, y, core: (1 - zh, y, core))
    up = device_pairs(lambda zh, y, core: (zh, (y + 1) % 4, core))
    down = device_pairs(lambda zh, y, core: (zh, (y - 1) % 4, core))
    across = device_pairs(lambda zh, y, core: (zh, (y + 2) % 4, core))

    given, kept = products(choice, lists, held, parts)
    arrived = moved(given, other_core)

    def quarter(step):
        at = ((y + step) % 4) * 4
        size = 4
        part = lax.dynamic_slice_in_dim(kept, at, size) + lax.dynamic_slice_in_dim(arrived, at, size)
        return part.reshape(size * TILE, TILE)

    with jax.named_scope("scatter_y"):
        sums = [
            moved(quarter(step).astype(jnp.bfloat16), pairs)
            for step, pairs in ((1, up), (3, down), (2, across))
        ]
        mine = quarter(0)
        for part in sums:
            mine = mine + part.astype(jnp.float32)
    with jax.named_scope("pair_z"):
        sent = mine.astype(jnp.bfloat16)
        back = moved(sent, other_half)
        aggregated = (sent.astype(jnp.float32) + back.astype(jnp.float32)).astype(jnp.bfloat16)
    with jax.named_scope("gather_y"):
        near = [aggregated] + [moved(aggregated, pairs) for pairs in (down, across, up)]
    with jax.named_scope("gather_core"):
        far = [moved(part, other_core) for part in near]
    return finished(near, far, weight, bias, y, core)


def finish_kernel(where, *refs):
    parts, (weight, bias, out, stage, sem) = refs[:8], refs[8:]
    y, core = where[0], where[1]
    rows = parts[0].shape[0]
    copies = []
    for n in range(8):
        slot = n % 4
        if n >= 4:
            copies[n - 4].wait()
        half = core if n < 4 else 1 - core
        quarter = (y + n) & 3
        result = jnp.dot(parts[n][...], weight[...], preferred_element_type=jnp.float32) + bias[...]
        stage[slot] = jnp.maximum(result, 0.0).astype(stage.dtype)
        start = pl.multiple_of((half * 4 + quarter) * rows, rows)
        copy = pltpu.make_async_copy(stage.at[slot], out.at[pl.ds(start, rows)], sem.at[slot])
        copy.start()
        copies.append(copy)
    for copy in copies[4:]:
        copy.wait()


def finished(near, far, weight, bias, y, core):
    vmem = pl.BlockSpec(memory_space=pltpu.VMEM)
    rows = near[0].shape[0]
    hidden = weight.shape[1]
    return pl.pallas_call(
        finish_kernel,
        out_shape=jax.ShapeDtypeStruct((8 * rows, hidden), jnp.bfloat16),
        in_specs=[pl.BlockSpec(memory_space=pltpu.SMEM)] + [vmem] * 10,
        out_specs=pl.BlockSpec(memory_space=pl.ANY),
        scratch_shapes=[
            pltpu.VMEM((4, rows, hidden), jnp.bfloat16),
            pltpu.SemaphoreType.DMA((4,)),
        ],
        compiler_params=pltpu.CompilerParams(vmem_limit_bytes=24 << 20),
        name="finish",
    )(jnp.stack([y, core]), *near, *far, weight, bias.reshape(1, hidden))


def solution(mesh):
    split = Mesh(mesh.devices.reshape(16, 2, 4, 2), AXES)
    rep = AXES[1:]
    in_specs = (
        P("blk", None),
        P(),
        P(),
        P("blk", rep, None, None, None),
        P("blk", rep, None),
        P("blk", rep),
    )
    return jax.shard_map(
        shards, mesh=split, in_specs=in_specs, out_specs=P("blk", None), check_vma=False
    )
```

```python
import jax
import jax.numpy as jnp
from jax import lax
from jax.experimental import pallas as pl
from jax.experimental.pallas import tpu as pltpu
from jax.sharding import Mesh
from jax.sharding import PartitionSpec as P

TILE = 128
ROW_TILES = 32
HALF_TILES = 16
SLOTS = 160
UNROLL = 8
AXES = ("blk", "zh", "y", "core")
LIST = 128
VMEM = pltpu.MemorySpace.VMEM

SOURCES = (
    (
        0x026474cf823a0156, 0x621a560f9802447d, 0x1304668efa2570ec, 0x01024fbe86456c8e,
        0x01423076cab8af98, 0x1047245f90a8cda8, 0x102644e98fbadec8, 0x67453ad8eecbcaf9,
        0x167324002e5d988e, 0x03041264f6abdaee, 0x1226760540bcde8e, 0x14052d0e6e8acafc,
        0x1043dc8f0725b98e, 0x002a8cf75129dace, 0x24cb8e7203a8d9fe, 0x0ad8f36165a84cbe,
    ),
    (
        0x0153826ae7d47513, 0x1152734dcfb5630e, 0x704313ac9d12659e, 0x13654dd8e0132bcf,
        0x620155318fec9adf, 0x13727018f6dd9fae, 0x1310365bdae98cff, 0x103157e798a9fddf,
        0x01355377d1b6eadb, 0x17527456301dfd9c, 0x161520373d8bf9fd, 0x0123476519acff8e,
        0x0735bfa82471ddf9, 0x1709cfa1875bedf9, 0x03f9bd5164cbfed9, 0x19abd4f309d3cbe8,
    ),
)
EXTRA = (
    (
        0x8023, 0x1841, 0x00a4, 0x0394, 0x1801, 0x4822, 0x0150, 0x0620,
        0x2290, 0x6049, 0x204a, 0x8884, 0x0140, 0x6005, 0x8801, 0x0c40,
    ),
    (
        0x420c, 0x0026, 0x0118, 0x0023, 0x0218, 0x0505, 0x4003, 0x3181,
        0x054e, 0x0c06, 0x1301, 0x1002, 0x1022, 0x00aa, 0x003c, 0x009a,
    ),
)


def feature_routes():
    routes = ([], [], [])
    taken = [0] * 256
    for chunk in range(2):
        for block in range(16):
            for section in range(16):
                replica = SOURCES[chunk][block] >> (4 * (15 - section)) & 15
                source = block * 16 + replica
                target = (block + section) % 16 * 16 + section
                if EXTRA[chunk][block] >> section & 1:
                    routes[2].append((source, target))
                    assert replica % 2 == chunk
                    taken[target] = 1 + chunk
                else:
                    routes[chunk].append((source, target))
    return routes, taken


def device_pairs(step):
    pairs = []
    for index in range(256):
        blk, rest = divmod(index, 16)
        zh, rest = divmod(rest, 8)
        y, core = divmod(rest, 2)
        zh, y, core = step(zh, y, core)
        pairs.append((index, blk * 16 + zh * 8 + y * 2 + core))
    return pairs


def moved(value, pairs):
    return lax.ppermute(value, AXES, pairs)


def split_kernel(features, first, second, extra, sems):
    rows = first.shape[0]
    core = lax.axis_index("core")
    copies = []
    for n, (start, piece) in enumerate(((0, first), (rows, second), (core * rows, extra))):
        copy = pltpu.make_async_copy(features.at[pl.ds(start, rows)], piece, sems.at[n])
        copy.start()
        copies.append(copy)
    for copy in copies:
        copy.wait()


def pieces_of(features):
    piece = pltpu.VMEM((features.shape[0] // 2, features.shape[1]), features.dtype)
    return pl.pallas_call(
        split_kernel,
        out_shape=(piece, piece, piece),
        in_specs=[pl.BlockSpec(memory_space=pltpu.HBM)],
        out_specs=(pl.BlockSpec(memory_space=pltpu.VMEM),) * 3,
        scratch_shapes=[pltpu.SemaphoreType.DMA((3,))],
        compiler_params=pltpu.CompilerParams(vmem_limit_bytes=1 << 20),
        name="split",
    )(pltpu.with_memory_space_constraint(features, pltpu.HBM))


def prepare_kernel(place, count, choice, tiles, held, slot_of, column_of, row_of, pairs, position, sem):
    total = count[0]
    fetch = pltpu.make_async_copy(tiles, held, sem)
    fetch.start()
    pairs[2] = choice[lax.axis_index(AXES)]

    for i in range(ROW_TILES + 1):
        position[i] = 0

    def number(k, carry):
        i = jnp.where(k < total, place[k] >> 5, ROW_TILES)
        position[i] = position[i] + 1
        return carry

    lax.fori_loop(0, SLOTS, number, 0, unroll=8)

    for half in range(2):
        first = half * LIST
        start = first
        for i in range(half * HALF_TILES, (half + 1) * HALF_TILES):
            n = position[i]
            position[i] = 2 * start
            start = start + ((n + 1) >> 1)
            last = jnp.where((n & 1) == 1, 2 * start - 1, 4 * LIST)
            slot_of[last] = 0
            column_of[last] = ROW_TILES
        pairs[half] = start - first
        for u in range(UNROLL - 1):
            row_of[start + u] = 0
            for v in range(2):
                slot_of[2 * (start + u) + v] = 0
                column_of[2 * (start + u) + v] = ROW_TILES
    position[ROW_TILES] = 4 * LIST + 8

    def lay(k, carry):
        p = place[k]
        i = jnp.where(k < total, p >> 5, ROW_TILES)
        q = position[i]
        position[i] = q + jnp.where(k < total, 1, 0)
        slot_of[q] = k
        column_of[q] = p & (ROW_TILES - 1)
        row_of[q >> 1] = i & (HALF_TILES - 1)
        return carry

    lax.fori_loop(0, SLOTS, lay, 0, unroll=8)
    fetch.wait()


def prepared(tiles, place, count, choice):
    smem = pl.BlockSpec(memory_space=pltpu.SMEM)
    return pl.pallas_call(
        prepare_kernel,
        out_shape=(
            pltpu.VMEM((SLOTS, TILE, TILE), tiles.dtype),
            jax.ShapeDtypeStruct((4 * LIST + 128,), jnp.int32),
            jax.ShapeDtypeStruct((4 * LIST + 128,), jnp.int32),
            jax.ShapeDtypeStruct((2 * LIST + 128,), jnp.int32),
            jax.ShapeDtypeStruct((3,), jnp.int32),
        ),
        in_specs=[smem, smem, smem, pl.BlockSpec(memory_space=pltpu.HBM)],
        out_specs=(pl.BlockSpec(memory_space=pltpu.VMEM), smem, smem, smem, smem),
        scratch_shapes=[pltpu.SMEM((ROW_TILES + 1,), jnp.int32), pltpu.SemaphoreType.DMA],
        cost_estimate=pl.CostEstimate(flops=0, bytes_accessed=16_000_000, transcendentals=0),
        compiler_params=pltpu.CompilerParams(vmem_limit_bytes=1 << 20),
        name="prepare",
    )(place, count, choice, pltpu.with_memory_space_constraint(tiles, pltpu.HBM))


def product_kernel(slot_of, column_of, row_of, pairs, held, first, second, extra, given, kept, source):
    core = lax.axis_index("core")
    taken = pairs[2]
    rows = HALF_TILES

    for chunk, plain in enumerate((first, second)):
        place = pl.ds(chunk * rows, rows)

        @pl.when(taken == 1 + chunk)
        def _():
            source[place] = extra[...]

        @pl.when(taken != 1 + chunk)
        def _():
            source[place] = plain[...]

    source[ROW_TILES] = jnp.zeros((TILE, TILE), source.dtype)

    for half, out in ((1 - core, given), (core, kept)):
        out[...] = jnp.zeros_like(out)
        base = half * LIST
        steps = (pairs[half] + UNROLL - 1) // UNROLL

        @pl.loop(0, steps)
        def _(step):
            start = base + step * UNROLL
            terms = []
            for u in range(UNROLL):
                q = 2 * (start + u)
                left = jnp.concatenate([held[slot_of[q]], held[slot_of[q + 1]]], axis=1)
                right = jnp.concatenate([source[column_of[q]], source[column_of[q + 1]]], axis=0)
                terms.append(jnp.dot(left, right, preferred_element_type=jnp.float32))
            for u in range(UNROLL):
                row = row_of[start + u]
                out[row] = out[row] + terms[u]


def products(lists, held, parts):
    smem = pl.BlockSpec(memory_space=pltpu.SMEM)
    vmem = pl.BlockSpec(memory_space=pltpu.VMEM)
    half = jax.ShapeDtypeStruct((HALF_TILES, TILE, TILE), jnp.float32)
    tiles = [part.reshape(HALF_TILES, TILE, TILE) for part in parts]
    return pl.pallas_call(
        product_kernel,
        out_shape=(half, half),
        in_specs=[smem] * 4 + [vmem] * 4,
        out_specs=(vmem, vmem),
        scratch_shapes=[pltpu.VMEM((ROW_TILES + 1, TILE, TILE), parts[0].dtype)],
        cost_estimate=pl.CostEstimate(flops=800_000_000, bytes_accessed=9_000_000, transcendentals=0),
        compiler_params=pltpu.CompilerParams(vmem_limit_bytes=8 << 20),
        name="products",
    )(*lists, held, *tiles)


def shards(features, weight, bias, tile_values, tile_place, tile_count):
    y = lax.axis_index("y")
    routes, taken = feature_routes()
    parts = [moved(piece, route) for piece, route in zip(pieces_of(features), routes)]
    held, *lists = prepared(
        tile_values[0, 0], tile_place[0, 0], tile_count[0], jnp.asarray(taken, jnp.int32)
    )

    other_core = device_pairs(lambda zh, y, core: (zh, y, 1 - core))
    other_half = device_pairs(lambda zh, y, core: (1 - zh, y, core))
    up = device_pairs(lambda zh, y, core: (zh, (y + 1) % 4, core))
    down = device_pairs(lambda zh, y, core: (zh, (y - 1) % 4, core))
    across = device_pairs(lambda zh, y, core: (zh, (y + 2) % 4, core))

    given, kept = products(lists, held, parts)
    arrived = moved(given, other_core)

    def quarter(step):
        at = ((y + step) % 4) * 4
        size = 4
        part = lax.dynamic_slice_in_dim(kept, at, size) + lax.dynamic_slice_in_dim(arrived, at, size)
        return part.reshape(size * TILE, TILE)

    with jax.named_scope("scatter_y"):
        sums = [
            moved(quarter(step).astype(jnp.bfloat16), pairs)
            for step, pairs in ((2, across), (1, up), (3, down))
        ]
        mine = quarter(0)
        for part in sums:
            mine = mine + part.astype(jnp.float32)
    with jax.named_scope("pair_z"):
        sent = mine.astype(jnp.bfloat16)
        back = moved(sent, other_half)
        aggregated = (sent.astype(jnp.float32) + back.astype(jnp.float32)).astype(jnp.bfloat16)
    with jax.named_scope("gather_y"):
        near = [aggregated] + [moved(aggregated, pairs) for pairs in (down, across, up)]
    with jax.named_scope("gather_core"):
        far = [moved(part, other_core) for part in near]
    return finished(near, far, weight, bias)


def finish_kernel(*refs):
    parts, (weight, bias, out, stage, sems) = refs[:8], refs[8:]
    y, core = lax.axis_index("y"), lax.axis_index("core")
    rows = parts[0].shape[0]
    copies = []
    for n in range(8):
        for m in range(0, rows, TILE):
            part = parts[n][m : m + TILE]
            result = jnp.dot(part, weight[...], preferred_element_type=jnp.float32) + bias[...]
            stage[n, m : m + TILE] = jnp.maximum(result, 0.0).astype(stage.dtype)
        half = core if n < 4 else 1 - core
        quarter = (y + n) & 3
        start = pl.multiple_of((half * 4 + quarter) * rows, rows)
        copy = pltpu.make_async_copy(stage.at[n], out.at[pl.ds(start, rows)], sems.at[n])
        copy.start()
        copies.append(copy)
    for copy in copies:
        copy.wait()


def finished(near, far, weight, bias):
    vmem = pl.BlockSpec(memory_space=pltpu.VMEM)
    rows = near[0].shape[0]
    hidden = weight.shape[1]
    return pl.pallas_call(
        finish_kernel,
        out_shape=jax.ShapeDtypeStruct((8 * rows, hidden), jnp.bfloat16),
        in_specs=[vmem] * 10,
        out_specs=pl.BlockSpec(memory_space=pl.ANY),
        scratch_shapes=[
            pltpu.VMEM((8, rows, hidden), jnp.bfloat16),
            pltpu.SemaphoreType.DMA((8,)),
        ],
        compiler_params=pltpu.CompilerParams(vmem_limit_bytes=24 << 20),
        name="finish",
    )(*near, *far, weight, bias.reshape(1, hidden))


def solution(mesh):
    split = Mesh(mesh.devices.reshape(16, 2, 4, 2), AXES)
    rep = AXES[1:]
    in_specs = (
        P("blk", None),
        P(),
        P(),
        P("blk", rep, None, None, None),
        P("blk", rep, None),
        P("blk", rep),
    )
    return jax.shard_map(
        shards, mesh=split, in_specs=in_specs, out_specs=P("blk", None), check_vma=False
    )
```

```python
import functools

import jax
import jax.numpy as jnp
from jax import lax
from jax.experimental import pallas as pl
from jax.experimental.pallas import tpu as pltpu
from jax.sharding import Mesh
from jax.sharding import PartitionSpec as P

TILE = 128
ROW_TILES = 32
HALF_TILES = 16
SLOTS = 160
UNROLL = 8
AXES = ("blk", "zh", "y", "core")
LIST = 128
VMEM = pltpu.MemorySpace.VMEM

SOURCES = (
    (
        0x0262684ec3a14507, 0x12025a6e8fc3470d, 0x140074a8cf6325eb, 0x07245d98e3016bcf,
        0x00234271efc98bad, 0x0144502e67a9edcf, 0x1256470ea9ed8bcf, 0x00532c6a4b8defc9,
        0x20526170af43cbe9, 0x0742146583abcdef, 0x0524061783c9ebad, 0x023154e069abcf8d,
        0x0442b8c96105adef, 0x304a9c05216feb8d, 0x05cbc27e61af4d89, 0x0ecc83712fa96deb,
    ),
    (
        0x3135d4f109eb6527, 0x16337508e9a1254f, 0x174313ec09256b8f, 0x01413b7ec9256d8f,
        0x16250357c9a3ed8f, 0x3710536729cbaf8d, 0x173241870fcbade9, 0x0613459faf8bc9ed,
        0x165043578721c9ed, 0x3134520fc169eb8d, 0x01425635e1abcd8f, 0x7715326a0bc9ed8f,
        0x07215dff47a3cde9, 0x163eb8d74529adcf, 0x0389bf1427a9cfed, 0x09a8d53721cb4def,
    ),
)
PERMUTES = (
    (
        0x2200202001010101, 0x1220100001010101, 0x1202100001010101, 0x2100111001010101,
        0x0221001101010101, 0x2120100201010101, 0x1010010201010101, 0x2011020001010101,
        0x0212011001010101, 0x0120100101010101, 0x2100001101010101, 0x2011100001010101,
        0x2022100101010101, 0x1200100101010101, 0x2101201001010101, 0x2202011101010101,
    ),
    (
        0x0022010210101010, 0x2102021110101010, 0x2010021110101010, 0x1012000110101010,
        0x2112120010101010, 0x0201021010101010, 0x2201101010101010, 0x1100102210101010,
        0x2121100210101010, 0x2201011010101010, 0x1211210010101010, 0x0200011110101010,
        0x1210022010101010, 0x0121012010101010, 0x1012020110101010, 0x1011200010101010,
    ),
)


def digit(word, section):
    return word >> (4 * (15 - section)) & 15


def feature_routes():
    routes = ([], [], [])
    carriers = [0] * 512
    for chunk in range(2):
        for block in range(16):
            for section in range(16):
                replica = digit(SOURCES[chunk][block], section)
                carrier = digit(PERMUTES[chunk][block], section)
                assert chunk == (replica + carrier) % 2
                target = (block + section) % 16 * 16 + section
                routes[carrier].append((block * 16 + replica, target))
                carriers[2 * target + chunk] = carrier
    return routes, carriers


def device_pairs(step):
    pairs = []
    for index in range(256):
        blk, rest = divmod(index, 16)
        zh, rest = divmod(rest, 8)
        y, core = divmod(rest, 2)
        zh, y, core = step(zh, y, core)
        pairs.append((index, blk * 16 + zh * 8 + y * 2 + core))
    return pairs


def moved(value, pairs):
    return lax.ppermute(value, AXES, pairs)


def split_kernel(features, same, other, sems):
    rows = same.shape[0]
    core = lax.axis_index("core")
    copies = []
    for n, (start, piece) in enumerate(((core * rows, same), ((1 - core) * rows, other))):
        copy = pltpu.make_async_copy(features.at[pl.ds(start, rows)], piece, sems.at[n])
        copy.start()
        copies.append(copy)
    for copy in copies:
        copy.wait()


def pieces_of(features):
    piece = pltpu.VMEM((features.shape[0] // 2, features.shape[1]), features.dtype)
    return pl.pallas_call(
        split_kernel,
        out_shape=(piece, piece),
        in_specs=[pl.BlockSpec(memory_space=pltpu.HBM)],
        out_specs=(pl.BlockSpec(memory_space=pltpu.VMEM),) * 2,
        scratch_shapes=[pltpu.SemaphoreType.DMA((2,))],
        compiler_params=pltpu.CompilerParams(vmem_limit_bytes=1 << 20),
        name="split",
    )(pltpu.with_memory_space_constraint(features, pltpu.HBM))


def prepare_kernel(place, count, choice, tiles, held, slot_of, column_of, row_of, pairs, position, sem):
    total = count[0]
    fetch = pltpu.make_async_copy(tiles, held, sem)
    fetch.start()
    me = lax.axis_index(AXES)
    pairs[2] = choice[2 * me]
    pairs[3] = choice[2 * me + 1]

    for i in range(ROW_TILES + 1):
        position[i] = 0

    def number(k, carry):
        i = jnp.where(k < total, place[k] >> 5, ROW_TILES)
        position[i] = position[i] + 1
        return carry

    lax.fori_loop(0, SLOTS, number, 0, unroll=8)

    for half in range(2):
        first = half * LIST
        start = first
        for i in range(half * HALF_TILES, (half + 1) * HALF_TILES):
            n = position[i]
            position[i] = 2 * start
            start = start + ((n + 1) >> 1)
            last = jnp.where((n & 1) == 1, 2 * start - 1, 4 * LIST)
            slot_of[last] = 0
            column_of[last] = ROW_TILES
        pairs[half] = start - first
        for u in range(UNROLL - 1):
            row_of[start + u] = 0
            for v in range(2):
                slot_of[2 * (start + u) + v] = 0
                column_of[2 * (start + u) + v] = ROW_TILES
    position[ROW_TILES] = 4 * LIST + 8

    def lay(k, carry):
        p = place[k]
        i = jnp.where(k < total, p >> 5, ROW_TILES)
        q = position[i]
        position[i] = q + jnp.where(k < total, 1, 0)
        slot_of[q] = k
        column_of[q] = p & (ROW_TILES - 1)
        row_of[q >> 1] = i & (HALF_TILES - 1)
        return carry

    lax.fori_loop(0, SLOTS, lay, 0, unroll=8)
    fetch.wait()


def prepared(tiles, place, count, choice):
    smem = pl.BlockSpec(memory_space=pltpu.SMEM)
    return pl.pallas_call(
        prepare_kernel,
        out_shape=(
            pltpu.VMEM((SLOTS, TILE, TILE), tiles.dtype),
            jax.ShapeDtypeStruct((4 * LIST + 128,), jnp.int32),
            jax.ShapeDtypeStruct((4 * LIST + 128,), jnp.int32),
            jax.ShapeDtypeStruct((2 * LIST + 128,), jnp.int32),
            jax.ShapeDtypeStruct((4,), jnp.int32),
        ),
        in_specs=[smem, smem, smem, pl.BlockSpec(memory_space=pltpu.HBM)],
        out_specs=(pl.BlockSpec(memory_space=pltpu.VMEM), smem, smem, smem, smem),
        scratch_shapes=[pltpu.SMEM((ROW_TILES + 1,), jnp.int32), pltpu.SemaphoreType.DMA],
        cost_estimate=pl.CostEstimate(flops=0, bytes_accessed=16_000_000, transcendentals=0),
        compiler_params=pltpu.CompilerParams(vmem_limit_bytes=1 << 20),
        name="prepare",
    )(place, count, choice, pltpu.with_memory_space_constraint(tiles, pltpu.HBM))


def product_kernel(slot_of, column_of, row_of, pairs, held, first, second, third, given, kept, source, total):
    core = lax.axis_index("core")
    for chunk in range(2):
        for carrier, part in enumerate((first, second, third)):

            @pl.when(pairs[2 + chunk] == carrier)
            def _():
                source[pl.ds(chunk * HALF_TILES, HALF_TILES)] = part[...]

    source[ROW_TILES] = jnp.zeros((TILE, TILE), source.dtype)

    for half, out in ((1 - core, total), (core, kept)):
        out[...] = jnp.zeros_like(out)
        base = half * LIST
        steps = (pairs[half] + UNROLL - 1) // UNROLL

        @pl.loop(0, steps)
        def _(step):
            start = base + step * UNROLL
            terms = []
            for u in range(UNROLL):
                q = 2 * (start + u)
                left = jnp.concatenate([held[slot_of[q]], held[slot_of[q + 1]]], axis=1)
                right = jnp.concatenate([source[column_of[q]], source[column_of[q + 1]]], axis=0)
                terms.append(jnp.dot(left, right, preferred_element_type=jnp.float32))
            for u in range(UNROLL):
                row = row_of[start + u]
                out[row] = out[row] + terms[u]

    given[...] = total[...].astype(given.dtype)


def products(lists, held, parts):
    smem = pl.BlockSpec(memory_space=pltpu.SMEM)
    vmem = pl.BlockSpec(memory_space=pltpu.VMEM)
    half = jax.ShapeDtypeStruct((HALF_TILES, TILE, TILE), jnp.float32)
    tiles = [part.reshape(HALF_TILES, TILE, TILE) for part in parts]
    return pl.pallas_call(
        product_kernel,
        out_shape=(jax.ShapeDtypeStruct(half.shape, jnp.bfloat16), half),
        in_specs=[smem] * 4 + [vmem] * 4,
        out_specs=(vmem, vmem),
        scratch_shapes=[
            pltpu.VMEM((ROW_TILES + 1, TILE, TILE), parts[0].dtype),
            pltpu.VMEM(half.shape, half.dtype),
        ],
        cost_estimate=pl.CostEstimate(flops=800_000_000, bytes_accessed=9_000_000, transcendentals=0),
        compiler_params=pltpu.CompilerParams(vmem_limit_bytes=8 << 20),
        name="products",
    )(*lists, held, *tiles)


def shards(features, weight, bias, tile_values, tile_place, tile_count):
    y = lax.axis_index("y")
    routes, carriers = feature_routes()
    same, other = pieces_of(features)
    parts = [moved(piece, route) for piece, route in zip((same, other, same), routes)]
    held, *lists = prepared(
        tile_values[0, 0], tile_place[0, 0], tile_count[0], jnp.asarray(carriers, jnp.int32)
    )

    other_core = device_pairs(lambda zh, y, core: (zh, y, 1 - core))
    other_half = device_pairs(lambda zh, y, core: (1 - zh, y, core))
    up = device_pairs(lambda zh, y, core: (zh, (y + 1) % 4, core))
    down = device_pairs(lambda zh, y, core: (zh, (y - 1) % 4, core))
    across = device_pairs(lambda zh, y, core: (zh, (y + 2) % 4, core))

    given, kept = products(lists, held, parts)
    arrived = moved(given, other_core)

    def quarter(step):
        at = ((y + step) % 4) * 4
        size = 4
        part = lax.dynamic_slice_in_dim(kept, at, size)
        part = part + lax.dynamic_slice_in_dim(arrived, at, size).astype(jnp.float32)
        return part.reshape(size * TILE, TILE)

    with jax.named_scope("scatter_y"):
        sums = [
            moved(quarter(step).astype(jnp.bfloat16), pairs)
            for step, pairs in ((2, across), (1, up), (3, down))
        ]
        mine = quarter(0)
        for part in sums:
            mine = mine + part.astype(jnp.float32)
    with jax.named_scope("pair_z"):
        sent = mine.astype(jnp.bfloat16)
        back = moved(sent, other_half)
        aggregated = (sent.astype(jnp.float32) + back.astype(jnp.float32)).astype(jnp.bfloat16)
    with jax.named_scope("gather_y"):
        near = [aggregated] + [moved(aggregated, pairs) for pairs in (down, across, up)]
    with jax.named_scope("gather_core"):
        far = [moved(part, other_core) for part in near]
    out = finished(near, weight, bias)
    return finished(far, weight, bias, out)


def finish_kernel(mine, *refs):
    (parts, weight, bias), (out, stage, sems) = (refs[:4], *refs[4:6]), refs[-3:]
    y, core = lax.axis_index("y"), lax.axis_index("core")
    rows = parts[0].shape[0]
    half = core if mine else 1 - core
    copies = []
    for n in range(4):
        for m in range(0, rows, TILE):
            part = parts[n][m : m + TILE]
            result = jnp.dot(part, weight[...], preferred_element_type=jnp.float32) + bias[...]
            stage[n, m : m + TILE] = jnp.maximum(result, 0.0).astype(stage.dtype)
        quarter = (y + n) & 3
        start = pl.multiple_of((half * 4 + quarter) * rows, rows)
        copy = pltpu.make_async_copy(stage.at[n], out.at[pl.ds(start, rows)], sems.at[n])
        copy.start()
        copies.append(copy)
    for copy in copies:
        copy.wait()


def finished(parts, weight, bias, out=None):
    vmem, hbm = pl.BlockSpec(memory_space=pltpu.VMEM), pl.BlockSpec(memory_space=pl.ANY)
    rows = parts[0].shape[0]
    hidden = weight.shape[1]
    first = out is None
    return pl.pallas_call(
        functools.partial(finish_kernel, first),
        out_shape=jax.ShapeDtypeStruct((8 * rows, hidden), jnp.bfloat16),
        in_specs=[vmem] * 6 + ([] if first else [hbm]),
        out_specs=hbm,
        scratch_shapes=[
            pltpu.VMEM((4, rows, hidden), jnp.bfloat16),
            pltpu.SemaphoreType.DMA((4,)),
        ],
        input_output_aliases={} if first else {6: 0},
        cost_estimate=pl.CostEstimate(flops=150_000_000, bytes_accessed=2_000_000, transcendentals=0),
        compiler_params=pltpu.CompilerParams(vmem_limit_bytes=16 << 20),
        name="finish",
    )(*parts, weight, bias.reshape(1, hidden), *([] if first else [out]))


def solution(mesh):
    split = Mesh(mesh.devices.reshape(16, 2, 4, 2), AXES)
    rep = AXES[1:]
    in_specs = (
        P("blk", None),
        P(),
        P(),
        P("blk", rep, None, None, None),
        P("blk", rep, None),
        P("blk", rep),
    )
    return jax.shard_map(
        shards, mesh=split, in_specs=in_specs, out_specs=P("blk", None), check_vma=False
    )
```

```python
import functools

import jax
import jax.numpy as jnp
from jax import lax
from jax.experimental import pallas as pl
from jax.experimental.pallas import tpu as pltpu
from jax.sharding import Mesh
from jax.sharding import PartitionSpec as P

TILE = 128
ROW_TILES = 32
HALF_TILES = 16
SLOTS = 160
UNROLL = 8
AXES = ("blk", "zh", "y", "core")
LIST = 128
VMEM = pltpu.MemorySpace.VMEM

SOURCES = (
    (
        0x0262684ec3a14507, 0x12025a6e8fc3470d, 0x140074a8cf6325eb, 0x07245d98e3016bcf,
        0x00234271efc98bad, 0x0144502e67a9edcf, 0x1256470ea9ed8bcf, 0x00532c6a4b8defc9,
        0x20526170af43cbe9, 0x0742146583abcdef, 0x0524061783c9ebad, 0x023154e069abcf8d,
        0x0442b8c96105adef, 0x304a9c05216feb8d, 0x05cbc27e61af4d89, 0x0ecc83712fa96deb,
    ),
    (
        0x3135d4f109eb6527, 0x16337508e9a1254f, 0x174313ec09256b8f, 0x01413b7ec9256d8f,
        0x16250357c9a3ed8f, 0x3710536729cbaf8d, 0x173241870fcbade9, 0x0613459faf8bc9ed,
        0x165043578721c9ed, 0x3134520fc169eb8d, 0x01425635e1abcd8f, 0x7715326a0bc9ed8f,
        0x07215dff47a3cde9, 0x163eb8d74529adcf, 0x0389bf1427a9cfed, 0x09a8d53721cb4def,
    ),
)
PERMUTES = (
    (
        0x2200202001010101, 0x1220100001010101, 0x1202100001010101, 0x2100111001010101,
        0x0221001101010101, 0x2120100201010101, 0x1010010201010101, 0x2011020001010101,
        0x0212011001010101, 0x0120100101010101, 0x2100001101010101, 0x2011100001010101,
        0x2022100101010101, 0x1200100101010101, 0x2101201001010101, 0x2202011101010101,
    ),
    (
        0x0022010210101010, 0x2102021110101010, 0x2010021110101010, 0x1012000110101010,
        0x2112120010101010, 0x0201021010101010, 0x2201101010101010, 0x1100102210101010,
        0x2121100210101010, 0x2201011010101010, 0x1211210010101010, 0x0200011110101010,
        0x1210022010101010, 0x0121012010101010, 0x1012020110101010, 0x1011200010101010,
    ),
)


def digit(word, section):
    return word >> (4 * (15 - section)) & 15


def feature_routes():
    routes = ([], [], [])
    carriers = [0] * 512
    for chunk in range(2):
        for block in range(16):
            for section in range(16):
                replica = digit(SOURCES[chunk][block], section)
                carrier = digit(PERMUTES[chunk][block], section)
                assert chunk == (replica + carrier) % 2
                target = (block + section) % 16 * 16 + section
                routes[carrier].append((block * 16 + replica, target))
                carriers[2 * target + chunk] = carrier
    return routes, carriers


def device_pairs(step):
    pairs = []
    for index in range(256):
        blk, rest = divmod(index, 16)
        zh, rest = divmod(rest, 8)
        y, core = divmod(rest, 2)
        zh, y, core = step(zh, y, core)
        pairs.append((index, blk * 16 + zh * 8 + y * 2 + core))
    return pairs


def moved(value, pairs):
    return lax.ppermute(value, AXES, pairs)


def split_kernel(features, same, other, sems):
    rows = same.shape[0]
    core = lax.axis_index("core")
    copies = []
    for n, (start, piece) in enumerate(((core * rows, same), ((1 - core) * rows, other))):
        copy = pltpu.make_async_copy(features.at[pl.ds(start, rows)], piece, sems.at[n])
        copy.start()
        copies.append(copy)
    for copy in copies:
        copy.wait()


def pieces_of(features):
    piece = pltpu.VMEM((features.shape[0] // 2, features.shape[1]), features.dtype)
    return pl.pallas_call(
        split_kernel,
        out_shape=(piece, piece),
        in_specs=[pl.BlockSpec(memory_space=pltpu.HBM)],
        out_specs=(pl.BlockSpec(memory_space=pltpu.VMEM),) * 2,
        scratch_shapes=[pltpu.SemaphoreType.DMA((2,))],
        compiler_params=pltpu.CompilerParams(vmem_limit_bytes=1 << 20),
        name="split",
    )(pltpu.with_memory_space_constraint(features, pltpu.HBM))


def prepare_kernel(place, count, choice, tiles, held, slot_of, column_of, row_of, facts, position, order, sem):
    total = count[0]
    fetch = pltpu.make_async_copy(tiles, held, sem)
    fetch.start()
    y = lax.axis_index("y")
    me = lax.axis_index(AXES)
    facts[1] = choice[2 * me]
    facts[2] = choice[2 * me + 1]

    for i in range(ROW_TILES + 1):
        position[i] = 0

    def number(k, carry):
        i = jnp.where(k < total, place[k] >> 5, ROW_TILES)
        position[i] = position[i] + 1
        return carry

    lax.fori_loop(0, SLOTS, number, 0, unroll=8)

    start = 0
    for i in range(ROW_TILES):
        n = position[i]
        position[i] = 2 * start
        start = start + ((n + 1) >> 1)
        last = jnp.where((n & 1) == 1, 2 * start - 1, 2 * LIST)
        slot_of[last] = 0
        column_of[last] = ROW_TILES
        step, within = ((i >> 3) - y) & 3, i & 7
        low, high = (8 + within, 12 + within) if within < 4 else (20 + within, 24 + within)
        order[i] = jnp.where(
            step == 1, within, jnp.where(step == 3, 16 + within, jnp.where(step == 2, low, high))
        )
    facts[0] = start
    for u in range(UNROLL - 1):
        row_of[start + u] = 0
        for v in range(2):
            slot_of[2 * (start + u) + v] = 0
            column_of[2 * (start + u) + v] = ROW_TILES
    position[ROW_TILES] = 2 * LIST + 8
    order[ROW_TILES] = 0

    def lay(k, carry):
        p = place[k]
        i = jnp.where(k < total, p >> 5, ROW_TILES)
        q = position[i]
        position[i] = q + jnp.where(k < total, 1, 0)
        slot_of[q] = k
        column_of[q] = p & (ROW_TILES - 1)
        row_of[q >> 1] = order[i]
        return carry

    lax.fori_loop(0, SLOTS, lay, 0, unroll=8)
    fetch.wait()


def prepared(tiles, place, count, choice):
    smem = pl.BlockSpec(memory_space=pltpu.SMEM)
    return pl.pallas_call(
        prepare_kernel,
        out_shape=(
            pltpu.VMEM((SLOTS, TILE, TILE), tiles.dtype),
            jax.ShapeDtypeStruct((2 * LIST + 128,), jnp.int32),
            jax.ShapeDtypeStruct((2 * LIST + 128,), jnp.int32),
            jax.ShapeDtypeStruct((LIST + 128,), jnp.int32),
            jax.ShapeDtypeStruct((3,), jnp.int32),
        ),
        in_specs=[smem, smem, smem, pl.BlockSpec(memory_space=pltpu.HBM)],
        out_specs=(pl.BlockSpec(memory_space=pltpu.VMEM), smem, smem, smem, smem),
        scratch_shapes=[
            pltpu.SMEM((ROW_TILES + 1,), jnp.int32),
            pltpu.SMEM((ROW_TILES + 1,), jnp.int32),
            pltpu.SemaphoreType.DMA,
        ],
        cost_estimate=pl.CostEstimate(flops=0, bytes_accessed=16_000_000, transcendentals=0),
        compiler_params=pltpu.CompilerParams(vmem_limit_bytes=1 << 20),
        name="prepare",
    )(place, count, choice, pltpu.with_memory_space_constraint(tiles, pltpu.HBM))


def product_kernel(slot_of, column_of, row_of, facts, held, first, second, third, given, total, source):
    core = lax.axis_index("core")
    for chunk in range(2):
        for carrier, part in enumerate((first, second, third)):

            @pl.when(facts[1 + chunk] == carrier)
            def _():
                source[pl.ds(chunk * HALF_TILES, HALF_TILES)] = part[...]

    source[ROW_TILES] = jnp.zeros((TILE, TILE), source.dtype)

    total[...] = jnp.zeros_like(total)
    steps = (facts[0] + UNROLL - 1) // UNROLL

    @pl.loop(0, steps)
    def _(step):
        start = step * UNROLL
        terms = []
        for u in range(UNROLL):
            q = 2 * (start + u)
            left = jnp.concatenate([held[slot_of[q]], held[slot_of[q + 1]]], axis=1)
            right = jnp.concatenate([source[column_of[q]], source[column_of[q + 1]]], axis=0)
            terms.append(jnp.dot(left, right, preferred_element_type=jnp.float32))
        for u in range(UNROLL):
            row = row_of[start + u]
            total[row] = total[row] + terms[u]

    given[...] = total[pl.ds((1 - core) * HALF_TILES, HALF_TILES)].astype(given.dtype)


def products(lists, held, parts):
    smem = pl.BlockSpec(memory_space=pltpu.SMEM)
    vmem = pl.BlockSpec(memory_space=pltpu.VMEM)
    tiles = [part.reshape(HALF_TILES, TILE, TILE) for part in parts]
    return pl.pallas_call(
        product_kernel,
        out_shape=(
            jax.ShapeDtypeStruct((HALF_TILES, TILE, TILE), jnp.bfloat16),
            jax.ShapeDtypeStruct((ROW_TILES, TILE, TILE), jnp.float32),
        ),
        in_specs=[smem] * 4 + [vmem] * 4,
        out_specs=(vmem, vmem),
        scratch_shapes=[pltpu.VMEM((ROW_TILES + 1, TILE, TILE), parts[0].dtype)],
        cost_estimate=pl.CostEstimate(flops=800_000_000, bytes_accessed=9_000_000, transcendentals=0),
        compiler_params=pltpu.CompilerParams(vmem_limit_bytes=8 << 20),
        name="products",
    )(*lists, held, *tiles)


def combine_kernel(total, arrived, near, far, mine):
    first = lax.axis_index("core") * HALF_TILES
    start = 0
    for out in (near, far, mine):
        size = out.shape[0]
        mid = total[pl.ds(first + start, size)] + arrived[start : start + size].astype(jnp.float32)
        out[...] = mid.astype(out.dtype)
        start += size


def combined(total, arrived):
    vmem = pl.BlockSpec(memory_space=pltpu.VMEM)
    part = HALF_TILES // 4
    return pl.pallas_call(
        combine_kernel,
        out_shape=(
            jax.ShapeDtypeStruct((2 * part, TILE, TILE), jnp.bfloat16),
            jax.ShapeDtypeStruct((part, TILE, TILE), jnp.bfloat16),
            jax.ShapeDtypeStruct((part, TILE, TILE), jnp.float32),
        ),
        in_specs=[vmem] * 2,
        out_specs=(vmem,) * 3,
        compiler_params=pltpu.CompilerParams(vmem_limit_bytes=8 << 20),
        name="combine",
    )(total, arrived)


def shards(features, weight, bias, tile_values, tile_place, tile_count):
    core = lax.axis_index("core")
    routes, carriers = feature_routes()
    same, other = pieces_of(features)
    parts = [moved(piece, route) for piece, route in zip((same, other, same), routes)]
    held, *lists = prepared(
        tile_values[0, 0], tile_place[0, 0], tile_count[0], jnp.asarray(carriers, jnp.int32)
    )

    other_core = device_pairs(lambda zh, y, core: (zh, y, 1 - core))
    other_half = device_pairs(lambda zh, y, core: (1 - zh, y, core))
    up = device_pairs(lambda zh, y, core: (zh, (y + 1) % 4, core))
    down = device_pairs(lambda zh, y, core: (zh, (y - 1) % 4, core))
    across = device_pairs(lambda zh, y, core: (zh, (y + 2) % 4, core))
    sideways = device_pairs(lambda zh, y, core: (zh, (y + 1 - 2 * core) % 4, core))

    given, total = products(lists, held, parts)
    arrived = moved(given, other_core)

    def rows_of(tiles):
        return tiles.reshape(-1, tiles.shape[-1])

    with jax.named_scope("scatter_y"):
        near, far, mine = (rows_of(part) for part in combined(total, arrived))
        part = far.shape[0]
        far = moved(far, across)
        near = moved(near, sideways)
        spare = moved(lax.dynamic_slice_in_dim(near, (1 - core) * part, part), other_core)
        for piece in (far, lax.dynamic_slice_in_dim(near, core * part, part), spare):
            mine = mine + piece.astype(jnp.float32)
    with jax.named_scope("pair_z"):
        sent = mine.astype(jnp.bfloat16)
        back = moved(sent, other_half)
        aggregated = (sent.astype(jnp.float32) + back.astype(jnp.float32)).astype(jnp.bfloat16)
    with jax.named_scope("gather_y"):
        near = [aggregated] + [moved(aggregated, pairs) for pairs in (down, across, up)]
    with jax.named_scope("gather_core"):
        far = [moved(part, other_core) for part in near]
    out = finished(near, weight, bias)
    return finished(far, weight, bias, out)


def finish_kernel(mine, *refs):
    (parts, weight, bias), (out, stage, sems) = (refs[:4], *refs[4:6]), refs[-3:]
    y, core = lax.axis_index("y"), lax.axis_index("core")
    rows = parts[0].shape[0]
    half = core if mine else 1 - core
    copies = []
    for n in range(4):
        for m in range(0, rows, TILE):
            part = parts[n][m : m + TILE]
            result = jnp.dot(part, weight[...], preferred_element_type=jnp.float32) + bias[...]
            stage[n, m : m + TILE] = jnp.maximum(result, 0.0).astype(stage.dtype)
        quarter = (y + n) & 3
        start = pl.multiple_of((quarter * 2 + half) * rows, rows)
        copy = pltpu.make_async_copy(stage.at[n], out.at[pl.ds(start, rows)], sems.at[n])
        copy.start()
        copies.append(copy)
    for copy in copies:
        copy.wait()


def finished(parts, weight, bias, out=None):
    vmem, hbm = pl.BlockSpec(memory_space=pltpu.VMEM), pl.BlockSpec(memory_space=pl.ANY)
    rows = parts[0].shape[0]
    hidden = weight.shape[1]
    first = out is None
    return pl.pallas_call(
        functools.partial(finish_kernel, first),
        out_shape=jax.ShapeDtypeStruct((8 * rows, hidden), jnp.bfloat16),
        in_specs=[vmem] * 6 + ([] if first else [hbm]),
        out_specs=hbm,
        scratch_shapes=[
            pltpu.VMEM((4, rows, hidden), jnp.bfloat16),
            pltpu.SemaphoreType.DMA((4,)),
        ],
        input_output_aliases={} if first else {6: 0},
        cost_estimate=pl.CostEstimate(flops=150_000_000, bytes_accessed=2_000_000, transcendentals=0),
        compiler_params=pltpu.CompilerParams(vmem_limit_bytes=16 << 20),
        name="finish",
    )(*parts, weight, bias.reshape(1, hidden), *([] if first else [out]))


def solution(mesh):
    split = Mesh(mesh.devices.reshape(16, 2, 4, 2), AXES)
    rep = AXES[1:]
    in_specs = (
        P("blk", None),
        P(),
        P(),
        P("blk", rep, None, None, None),
        P("blk", rep, None),
        P("blk", rep),
    )
    return jax.shard_map(
        shards, mesh=split, in_specs=in_specs, out_specs=P("blk", None), check_vma=False
    )
```

```python
import functools

import jax
import jax.numpy as jnp
from jax import lax
from jax.experimental import pallas as pl
from jax.experimental.pallas import tpu as pltpu
from jax.sharding import Mesh
from jax.sharding import PartitionSpec as P

TILE = 128
ROW_TILES = 32
HALF_TILES = 16
SLOTS = 160
UNROLL = 8
AXES = ("blk", "zh", "y", "core")
LIST = 128
VMEM = pltpu.MemorySpace.VMEM

SOURCES = (
    (
        0x0262684ec3a14507, 0x12025a6e8fc3470d, 0x140074a8cf6325eb, 0x07245d98e3016bcf,
        0x00234271efc98bad, 0x0144502e67a9edcf, 0x1256470ea9ed8bcf, 0x00532c6a4b8defc9,
        0x20526170af43cbe9, 0x0742146583abcdef, 0x0524061783c9ebad, 0x023154e069abcf8d,
        0x0442b8c96105adef, 0x304a9c05216feb8d, 0x05cbc27e61af4d89, 0x0ecc83712fa96deb,
    ),
    (
        0x3135d4f109eb6527, 0x16337508e9a1254f, 0x174313ec09256b8f, 0x01413b7ec9256d8f,
        0x16250357c9a3ed8f, 0x3710536729cbaf8d, 0x173241870fcbade9, 0x0613459faf8bc9ed,
        0x165043578721c9ed, 0x3134520fc169eb8d, 0x01425635e1abcd8f, 0x7715326a0bc9ed8f,
        0x07215dff47a3cde9, 0x163eb8d74529adcf, 0x0389bf1427a9cfed, 0x09a8d53721cb4def,
    ),
)
PERMUTES = (
    (
        0x2200202001010101, 0x1220100001010101, 0x1202100001010101, 0x2100111001010101,
        0x0221001101010101, 0x2120100201010101, 0x1010010201010101, 0x2011020001010101,
        0x0212011001010101, 0x0120100101010101, 0x2100001101010101, 0x2011100001010101,
        0x2022100101010101, 0x1200100101010101, 0x2101201001010101, 0x2202011101010101,
    ),
    (
        0x0022010210101010, 0x2102021110101010, 0x2010021110101010, 0x1012000110101010,
        0x2112120010101010, 0x0201021010101010, 0x2201101010101010, 0x1100102210101010,
        0x2121100210101010, 0x2201011010101010, 0x1211210010101010, 0x0200011110101010,
        0x1210022010101010, 0x0121012010101010, 0x1012020110101010, 0x1011200010101010,
    ),
)


def digit(word, section):
    return word >> (4 * (15 - section)) & 15


def feature_routes():
    routes = ([], [], [])
    carriers = [0] * 512
    for chunk in range(2):
        for block in range(16):
            for section in range(16):
                replica = digit(SOURCES[chunk][block], section)
                carrier = digit(PERMUTES[chunk][block], section)
                assert chunk == (replica + carrier) % 2
                target = (block + section) % 16 * 16 + section
                routes[carrier].append((block * 16 + replica, target))
                carriers[2 * target + chunk] = carrier
    return routes, carriers


def device_pairs(step):
    pairs = []
    for index in range(256):
        blk, rest = divmod(index, 16)
        zh, rest = divmod(rest, 8)
        y, core = divmod(rest, 2)
        zh, y, core = step(zh, y, core)
        pairs.append((index, blk * 16 + zh * 8 + y * 2 + core))
    return pairs


def moved(value, pairs):
    return lax.ppermute(value, AXES, pairs)


def split_kernel(features, same, other, sems):
    rows = same.shape[0]
    core = lax.axis_index("core")
    copies = []
    for n, (start, piece) in enumerate(((core * rows, same), ((1 - core) * rows, other))):
        copy = pltpu.make_async_copy(features.at[pl.ds(start, rows)], piece, sems.at[n])
        copy.start()
        copies.append(copy)
    for copy in copies:
        copy.wait()


def pieces_of(features):
    piece = pltpu.VMEM((features.shape[0] // 2, features.shape[1]), features.dtype)
    return pl.pallas_call(
        split_kernel,
        out_shape=(piece, piece),
        in_specs=[pl.BlockSpec(memory_space=pltpu.HBM)],
        out_specs=(pl.BlockSpec(memory_space=pltpu.VMEM),) * 2,
        scratch_shapes=[pltpu.SemaphoreType.DMA((2,))],
        compiler_params=pltpu.CompilerParams(vmem_limit_bytes=1 << 20),
        name="split",
    )(pltpu.with_memory_space_constraint(features, pltpu.HBM))


def prepare_kernel(
    place, count, choice, tiles, early, late, slot_of, column_of, row_of, facts, position, order, sems
):
    total = count[0]
    fetches = []
    for n, held in enumerate((early, late)):
        fetch = pltpu.make_async_copy(tiles, held.at[pl.ds(0, SLOTS)], sems.at[n])
        fetch.start()
        fetches.append(fetch)
        held[SLOTS] = jnp.zeros((TILE, TILE), held.dtype)
    y = lax.axis_index("y")
    me = lax.axis_index(AXES)
    facts[2] = choice[2 * me]
    facts[3] = choice[2 * me + 1]
    wait = [jnp.where(choice[2 * me + chunk] == 1, ROW_TILES, 0) for chunk in range(2)]

    def key_of(k):
        p = place[k]
        key = (p >> 5) + jnp.where(((p >> 4) & 1) == 1, wait[1], wait[0])
        return jnp.where(k < total, key, 2 * ROW_TILES), p

    for i in range(2 * ROW_TILES + 1):
        position[i] = 0

    def number(k, carry):
        i, _ = key_of(k)
        position[i] = position[i] + 1
        return carry

    lax.fori_loop(0, SLOTS, number, 0, unroll=8)

    for i in range(ROW_TILES):
        step, within = ((i >> 3) - y) & 3, i & 7
        low, high = (8 + within, 12 + within) if within < 4 else (20 + within, 24 + within)
        order[i] = jnp.where(
            step == 1, within, jnp.where(step == 3, 16 + within, jnp.where(step == 2, low, high))
        )
    for group in range(2):
        start = group * LIST
        for i in range(group * ROW_TILES, (group + 1) * ROW_TILES):
            n = position[i]
            position[i] = 2 * start
            start = start + ((n + 1) >> 1)
            last = jnp.where((n & 1) == 1, 2 * start - 1, 4 * LIST)
            slot_of[last] = SLOTS
            column_of[last] = 0
        facts[group] = start - group * LIST
        for u in range(UNROLL - 1):
            row_of[start + u] = 0
            for v in range(2):
                slot_of[2 * (start + u) + v] = SLOTS
                column_of[2 * (start + u) + v] = 0
    position[2 * ROW_TILES] = 4 * LIST + 8

    def lay(k, carry):
        i, p = key_of(k)
        q = position[i]
        position[i] = q + jnp.where(k < total, 1, 0)
        slot_of[q] = k
        column_of[q] = p & (ROW_TILES - 1)
        row_of[q >> 1] = order[i & (ROW_TILES - 1)]
        return carry

    lax.fori_loop(0, SLOTS, lay, 0, unroll=8)
    for fetch in fetches:
        fetch.wait()


def prepared(tiles, place, count, choice):
    smem, vmem = pl.BlockSpec(memory_space=pltpu.SMEM), pl.BlockSpec(memory_space=pltpu.VMEM)
    held = pltpu.VMEM((SLOTS + 1, TILE, TILE), tiles.dtype)
    return pl.pallas_call(
        prepare_kernel,
        out_shape=(
            held,
            held,
            jax.ShapeDtypeStruct((4 * LIST + 128,), jnp.int32),
            jax.ShapeDtypeStruct((4 * LIST + 128,), jnp.int32),
            jax.ShapeDtypeStruct((2 * LIST + 128,), jnp.int32),
            jax.ShapeDtypeStruct((4,), jnp.int32),
        ),
        in_specs=[smem, smem, smem, pl.BlockSpec(memory_space=pltpu.HBM)],
        out_specs=(vmem, vmem, smem, smem, smem, smem),
        scratch_shapes=[
            pltpu.SMEM((2 * ROW_TILES + 1,), jnp.int32),
            pltpu.SMEM((ROW_TILES,), jnp.int32),
            pltpu.SemaphoreType.DMA((2,)),
        ],
        cost_estimate=pl.CostEstimate(flops=0, bytes_accessed=16_000_000, transcendentals=0),
        compiler_params=pltpu.CompilerParams(vmem_limit_bytes=1 << 20),
        name="prepare",
    )(place, count, choice, pltpu.with_memory_space_constraint(tiles, pltpu.HBM))


def add_products(group, mask, slot_of, column_of, row_of, facts, held, source, total):
    steps = (facts[group] + UNROLL - 1) // UNROLL

    @pl.loop(0, steps)
    def _(step):
        start = group * LIST + step * UNROLL
        terms = []
        for u in range(UNROLL):
            q = 2 * (start + u)
            left = jnp.concatenate([held[slot_of[q]], held[slot_of[q + 1]]], axis=1)
            columns = [source[column_of[q + v] & mask] for v in range(2)]
            right = jnp.concatenate(columns, axis=0)
            terms.append(jnp.dot(left, right, preferred_element_type=jnp.float32))
        for u in range(UNROLL):
            row = row_of[start + u]
            total[row] = total[row] + terms[u]


def early_kernel(slot_of, column_of, row_of, facts, held, first, third, total, source):
    for chunk in range(2):
        for carrier, part in ((0, first), (2, third)):

            @pl.when(facts[2 + chunk] == carrier)
            def _():
                source[pl.ds(chunk * HALF_TILES, HALF_TILES)] = part[...]

        @pl.when(facts[2 + chunk] == 1)
        def _():
            source[pl.ds(chunk * HALF_TILES, HALF_TILES)] = jnp.zeros_like(first)

    total[...] = jnp.zeros_like(total)
    add_products(0, ROW_TILES - 1, slot_of, column_of, row_of, facts, held, source, total)


def late_kernel(slot_of, column_of, row_of, facts, held, second, before, total, given):
    del before
    core = lax.axis_index("core")
    add_products(1, HALF_TILES - 1, slot_of, column_of, row_of, facts, held, second, total)
    given[...] = total[pl.ds((1 - core) * HALF_TILES, HALF_TILES)].astype(given.dtype)


def products(lists, early, late, parts):
    smem = pl.BlockSpec(memory_space=pltpu.SMEM)
    vmem = pl.BlockSpec(memory_space=pltpu.VMEM)
    first, second, third = (part.reshape(HALF_TILES, TILE, TILE) for part in parts)
    sums = jax.ShapeDtypeStruct((ROW_TILES, TILE, TILE), jnp.float32)
    half = jax.ShapeDtypeStruct((HALF_TILES, TILE, TILE), jnp.bfloat16)
    cost = pl.CostEstimate(flops=400_000_000, bytes_accessed=9_000_000, transcendentals=0)
    limit = pltpu.CompilerParams(vmem_limit_bytes=8 << 20)
    total = pl.pallas_call(
        early_kernel,
        out_shape=sums,
        in_specs=[smem] * 4 + [vmem] * 3,
        out_specs=vmem,
        scratch_shapes=[pltpu.VMEM((ROW_TILES, TILE, TILE), first.dtype)],
        cost_estimate=cost,
        compiler_params=limit,
        name="early_products",
    )(*lists, early, first, third)
    return pl.pallas_call(
        late_kernel,
        out_shape=(sums, half),
        in_specs=[smem] * 4 + [vmem] * 3,
        out_specs=(vmem, vmem),
        input_output_aliases={6: 0},
        cost_estimate=cost,
        compiler_params=limit,
        name="late_products",
    )(*lists, late, second, total)


def combine_kernel(total, arrived, near, far, mine):
    first = lax.axis_index("core") * HALF_TILES
    start = 0
    for out in (near, far, mine):
        size = out.shape[0]
        mid = total[pl.ds(first + start, size)] + arrived[start : start + size].astype(jnp.float32)
        out[...] = mid.astype(out.dtype)
        start += size


def combined(total, arrived):
    vmem = pl.BlockSpec(memory_space=pltpu.VMEM)
    part = HALF_TILES // 4
    return pl.pallas_call(
        combine_kernel,
        out_shape=(
            jax.ShapeDtypeStruct((2 * part, TILE, TILE), jnp.bfloat16),
            jax.ShapeDtypeStruct((part, TILE, TILE), jnp.bfloat16),
            jax.ShapeDtypeStruct((part, TILE, TILE), jnp.float32),
        ),
        in_specs=[vmem] * 2,
        out_specs=(vmem,) * 3,
        compiler_params=pltpu.CompilerParams(vmem_limit_bytes=8 << 20),
        name="combine",
    )(total, arrived)


def shards(features, weight, bias, tile_values, tile_place, tile_count):
    core = lax.axis_index("core")
    routes, carriers = feature_routes()
    same, other = pieces_of(features)
    parts = [moved(piece, route) for piece, route in zip((same, other, same), routes)]
    early, late, *lists = prepared(
        tile_values[0, 0], tile_place[0, 0], tile_count[0], jnp.asarray(carriers, jnp.int32)
    )

    other_core = device_pairs(lambda zh, y, core: (zh, y, 1 - core))
    other_half = device_pairs(lambda zh, y, core: (1 - zh, y, core))
    up = device_pairs(lambda zh, y, core: (zh, (y + 1) % 4, core))
    down = device_pairs(lambda zh, y, core: (zh, (y - 1) % 4, core))
    across = device_pairs(lambda zh, y, core: (zh, (y + 2) % 4, core))
    sideways = device_pairs(lambda zh, y, core: (zh, (y + 1 - 2 * core) % 4, core))

    total, given = products(lists, early, late, parts)
    arrived = moved(given, other_core)

    def rows_of(tiles):
        return tiles.reshape(-1, tiles.shape[-1])

    with jax.named_scope("scatter_y"):
        near, far, mine = (rows_of(part) for part in combined(total, arrived))
        part = far.shape[0]
        far = moved(far, across)
        near = moved(near, sideways)
        spare = moved(lax.dynamic_slice_in_dim(near, (1 - core) * part, part), other_core)
        for piece in (far, lax.dynamic_slice_in_dim(near, core * part, part), spare):
            mine = mine + piece.astype(jnp.float32)
    with jax.named_scope("pair_z"):
        sent = mine.astype(jnp.bfloat16)
        back = moved(sent, other_half)
        aggregated = (sent.astype(jnp.float32) + back.astype(jnp.float32)).astype(jnp.bfloat16)
    with jax.named_scope("gather_y"):
        near = [aggregated] + [moved(aggregated, pairs) for pairs in (down, across, up)]
    with jax.named_scope("gather_core"):
        far = [moved(part, other_core) for part in near]
    out = finished(near, weight, bias)
    return finished(far, weight, bias, out)


def finish_kernel(mine, *refs):
    (parts, weight, bias), (out, stage, sems) = (refs[:4], *refs[4:6]), refs[-3:]
    y, core = lax.axis_index("y"), lax.axis_index("core")
    rows = parts[0].shape[0]
    half = core if mine else 1 - core
    copies = []
    for n in range(4):
        for m in range(0, rows, TILE):
            part = parts[n][m : m + TILE]
            result = jnp.dot(part, weight[...], preferred_element_type=jnp.float32) + bias[...]
            stage[n, m : m + TILE] = jnp.maximum(result, 0.0).astype(stage.dtype)
        quarter = (y + n) & 3
        start = pl.multiple_of((quarter * 2 + half) * rows, rows)
        copy = pltpu.make_async_copy(stage.at[n], out.at[pl.ds(start, rows)], sems.at[n])
        copy.start()
        copies.append(copy)
    for copy in copies:
        copy.wait()


def finished(parts, weight, bias, out=None):
    vmem, hbm = pl.BlockSpec(memory_space=pltpu.VMEM), pl.BlockSpec(memory_space=pl.ANY)
    rows = parts[0].shape[0]
    hidden = weight.shape[1]
    first = out is None
    return pl.pallas_call(
        functools.partial(finish_kernel, first),
        out_shape=jax.ShapeDtypeStruct((8 * rows, hidden), jnp.bfloat16),
        in_specs=[vmem] * 6 + ([] if first else [hbm]),
        out_specs=hbm,
        scratch_shapes=[
            pltpu.VMEM((4, rows, hidden), jnp.bfloat16),
            pltpu.SemaphoreType.DMA((4,)),
        ],
        input_output_aliases={} if first else {6: 0},
        cost_estimate=pl.CostEstimate(flops=150_000_000, bytes_accessed=2_000_000, transcendentals=0),
        compiler_params=pltpu.CompilerParams(vmem_limit_bytes=16 << 20),
        name="finish",
    )(*parts, weight, bias.reshape(1, hidden), *([] if first else [out]))


def solution(mesh):
    split = Mesh(mesh.devices.reshape(16, 2, 4, 2), AXES)
    rep = AXES[1:]
    in_specs = (
        P("blk", None),
        P(),
        P(),
        P("blk", rep, None, None, None),
        P("blk", rep, None),
        P("blk", rep),
    )
    return jax.shard_map(
        shards, mesh=split, in_specs=in_specs, out_specs=P("blk", None), check_vma=False
    )
```

```python
import functools

import jax
import jax.numpy as jnp
from jax import lax
from jax.experimental import pallas as pl
from jax.experimental.pallas import tpu as pltpu
from jax.sharding import Mesh
from jax.sharding import PartitionSpec as P

TILE = 128
ROW_TILES = 32
HALF_TILES = 16
SLOTS = 160
UNROLL = 8
AXES = ("blk", "zh", "y", "core")
LIST = 128
VMEM = pltpu.MemorySpace.VMEM

SOURCES = (
    (
        0x0262684ec3a14507, 0x12025a6e8fc3470d, 0x140074a8cf6325eb, 0x07245d98e3016bcf,
        0x00234271efc98bad, 0x0144502e67a9edcf, 0x1256470ea9ed8bcf, 0x00532c6a4b8defc9,
        0x20526170af43cbe9, 0x0742146583abcdef, 0x0524061783c9ebad, 0x023154e069abcf8d,
        0x0442b8c96105adef, 0x304a9c05216feb8d, 0x05cbc27e61af4d89, 0x0ecc83712fa96deb,
    ),
    (
        0x3135d4f109eb6527, 0x16337508e9a1254f, 0x174313ec09256b8f, 0x01413b7ec9256d8f,
        0x16250357c9a3ed8f, 0x3710536729cbaf8d, 0x173241870fcbade9, 0x0613459faf8bc9ed,
        0x165043578721c9ed, 0x3134520fc169eb8d, 0x01425635e1abcd8f, 0x7715326a0bc9ed8f,
        0x07215dff47a3cde9, 0x163eb8d74529adcf, 0x0389bf1427a9cfed, 0x09a8d53721cb4def,
    ),
)
PERMUTES = (
    (
        0x2200202001010101, 0x1220100001010101, 0x1202100001010101, 0x2100111001010101,
        0x0221001101010101, 0x2120100201010101, 0x1010010201010101, 0x2011020001010101,
        0x0212011001010101, 0x0120100101010101, 0x2100001101010101, 0x2011100001010101,
        0x2022100101010101, 0x1200100101010101, 0x2101201001010101, 0x2202011101010101,
    ),
    (
        0x0022010210101010, 0x2102021110101010, 0x2010021110101010, 0x1012000110101010,
        0x2112120010101010, 0x0201021010101010, 0x2201101010101010, 0x1100102210101010,
        0x2121100210101010, 0x2201011010101010, 0x1211210010101010, 0x0200011110101010,
        0x1210022010101010, 0x0121012010101010, 0x1012020110101010, 0x1011200010101010,
    ),
)


def digit(word, section):
    return word >> (4 * (15 - section)) & 15


def feature_routes():
    routes = ([], [], [])
    carriers = [0] * 512
    for chunk in range(2):
        for block in range(16):
            for section in range(16):
                replica = digit(SOURCES[chunk][block], section)
                carrier = digit(PERMUTES[chunk][block], section)
                assert chunk == (replica + carrier) % 2
                target = (block + section) % 16 * 16 + section
                routes[carrier].append((block * 16 + replica, target))
                carriers[2 * target + chunk] = carrier
    return routes, carriers


def device_pairs(step):
    pairs = []
    for index in range(256):
        blk, rest = divmod(index, 16)
        zh, rest = divmod(rest, 8)
        y, core = divmod(rest, 2)
        zh, y, core = step(zh, y, core)
        pairs.append((index, blk * 16 + zh * 8 + y * 2 + core))
    return pairs


def moved(value, pairs):
    return lax.ppermute(value, AXES, pairs)


def split_kernel(features, same, other, sems):
    rows = same.shape[0]
    core = lax.axis_index("core")
    copies = []
    for n, (start, piece) in enumerate(((core * rows, same), ((1 - core) * rows, other))):
        copy = pltpu.make_async_copy(features.at[pl.ds(start, rows)], piece, sems.at[n])
        copy.start()
        copies.append(copy)
    for copy in copies:
        copy.wait()


def pieces_of(features):
    piece = pltpu.VMEM((features.shape[0] // 2, features.shape[1]), features.dtype)
    return pl.pallas_call(
        split_kernel,
        out_shape=(piece, piece),
        in_specs=[pl.BlockSpec(memory_space=pltpu.HBM)],
        out_specs=(pl.BlockSpec(memory_space=pltpu.VMEM),) * 2,
        scratch_shapes=[pltpu.SemaphoreType.DMA((2,))],
        compiler_params=pltpu.CompilerParams(vmem_limit_bytes=1 << 20),
        name="split",
    )(pltpu.with_memory_space_constraint(features, pltpu.HBM))


def prepare_kernel(place, count, choice, tiles, held, slot_of, column_of, row_of, facts, position, sem):
    total = count[0]
    fetch = pltpu.make_async_copy(tiles, held, sem)
    fetch.start()
    me = lax.axis_index(AXES)
    facts[1] = choice[2 * me]
    facts[2] = choice[2 * me + 1]

    for i in range(ROW_TILES + 1):
        position[i] = 0

    def number(k, carry):
        i = jnp.where(k < total, place[k] >> 5, ROW_TILES)
        position[i] = position[i] + 1
        return carry

    lax.fori_loop(0, SLOTS, number, 0, unroll=8)

    start = 0
    for i in range(ROW_TILES):
        n = position[i]
        position[i] = 2 * start
        start = start + ((n + 1) >> 1)
        last = jnp.where((n & 1) == 1, 2 * start - 1, 2 * LIST)
        slot_of[last] = 0
        column_of[last] = ROW_TILES
    facts[0] = start
    for u in range(UNROLL - 1):
        row_of[start + u] = 0
        for v in range(2):
            slot_of[2 * (start + u) + v] = 0
            column_of[2 * (start + u) + v] = ROW_TILES
    position[ROW_TILES] = 2 * LIST + 8

    def lay(k, carry):
        p = place[k]
        i = jnp.where(k < total, p >> 5, ROW_TILES)
        q = position[i]
        position[i] = q + jnp.where(k < total, 1, 0)
        slot_of[q] = k
        column_of[q] = p & (ROW_TILES - 1)
        row_of[q >> 1] = i & (ROW_TILES - 1)
        return carry

    lax.fori_loop(0, SLOTS, lay, 0, unroll=8)
    fetch.wait()


def prepared(tiles, place, count, choice):
    smem = pl.BlockSpec(memory_space=pltpu.SMEM)
    return pl.pallas_call(
        prepare_kernel,
        out_shape=(
            pltpu.VMEM((SLOTS, TILE, TILE), tiles.dtype),
            jax.ShapeDtypeStruct((2 * LIST + 128,), jnp.int32),
            jax.ShapeDtypeStruct((2 * LIST + 128,), jnp.int32),
            jax.ShapeDtypeStruct((LIST + 128,), jnp.int32),
            jax.ShapeDtypeStruct((3,), jnp.int32),
        ),
        in_specs=[smem, smem, smem, pl.BlockSpec(memory_space=pltpu.HBM)],
        out_specs=(pl.BlockSpec(memory_space=pltpu.VMEM), smem, smem, smem, smem),
        scratch_shapes=[
            pltpu.SMEM((ROW_TILES + 1,), jnp.int32),
            pltpu.SemaphoreType.DMA,
        ],
        cost_estimate=pl.CostEstimate(flops=0, bytes_accessed=16_000_000, transcendentals=0),
        compiler_params=pltpu.CompilerParams(vmem_limit_bytes=1 << 20),
        name="prepare",
    )(place, count, choice, pltpu.with_memory_space_constraint(tiles, pltpu.HBM))


def product_kernel(slot_of, column_of, row_of, facts, held, first, second, third, given, total, source):
    core = lax.axis_index("core")
    for chunk in range(2):
        for carrier, part in enumerate((first, second, third)):

            @pl.when(facts[1 + chunk] == carrier)
            def _():
                source[pl.ds(chunk * HALF_TILES, HALF_TILES)] = part[...]

    source[ROW_TILES] = jnp.zeros((TILE, TILE), source.dtype)

    total[...] = jnp.zeros_like(total)
    steps = (facts[0] + UNROLL - 1) // UNROLL

    @pl.loop(0, steps)
    def _(step):
        start = step * UNROLL
        terms = []
        for u in range(UNROLL):
            q = 2 * (start + u)
            left = jnp.concatenate([held[slot_of[q]], held[slot_of[q + 1]]], axis=1)
            right = jnp.concatenate([source[column_of[q]], source[column_of[q + 1]]], axis=0)
            terms.append(jnp.dot(left, right, preferred_element_type=jnp.float32))
        for u in range(UNROLL):
            row = row_of[start + u]
            total[row] = total[row] + terms[u]

    given[...] = total[pl.ds((1 - core) * HALF_TILES, HALF_TILES)].astype(given.dtype)


def products(lists, held, parts):
    smem = pl.BlockSpec(memory_space=pltpu.SMEM)
    vmem = pl.BlockSpec(memory_space=pltpu.VMEM)
    tiles = [part.reshape(HALF_TILES, TILE, TILE) for part in parts]
    return pl.pallas_call(
        product_kernel,
        out_shape=(
            jax.ShapeDtypeStruct((HALF_TILES, TILE, TILE), jnp.bfloat16),
            jax.ShapeDtypeStruct((ROW_TILES, TILE, TILE), jnp.float32),
        ),
        in_specs=[smem] * 4 + [vmem] * 4,
        out_specs=(vmem, vmem),
        scratch_shapes=[pltpu.VMEM((ROW_TILES + 1, TILE, TILE), parts[0].dtype)],
        cost_estimate=pl.CostEstimate(flops=800_000_000, bytes_accessed=9_000_000, transcendentals=0),
        compiler_params=pltpu.CompilerParams(vmem_limit_bytes=8 << 20),
        name="products",
    )(*lists, held, *tiles)


def shards(features, weight, bias, tile_values, tile_place, tile_count):
    y, core = lax.axis_index("y"), lax.axis_index("core")
    routes, carriers = feature_routes()
    same, other = pieces_of(features)
    parts = [moved(piece, route) for piece, route in zip((same, other, same), routes)]
    held, *lists = prepared(
        tile_values[0, 0], tile_place[0, 0], tile_count[0], jnp.asarray(carriers, jnp.int32)
    )

    other_core = device_pairs(lambda zh, y, core: (zh, y, 1 - core))
    other_half = device_pairs(lambda zh, y, core: (1 - zh, y, core))
    up = device_pairs(lambda zh, y, core: (zh, (y + 1) % 4, core))
    down = device_pairs(lambda zh, y, core: (zh, (y - 1) % 4, core))
    across = device_pairs(lambda zh, y, core: (zh, (y + 2) % 4, core))

    given, total = products(lists, held, parts)
    arrived = moved(given, other_core)

    def quarter(step):
        at = ((y + step) % 4) * 4
        size = 4
        part = lax.dynamic_slice_in_dim(total, core * HALF_TILES + at, size)
        part = part + lax.dynamic_slice_in_dim(arrived, at, size).astype(jnp.float32)
        return part.reshape(size * TILE, TILE)

    with jax.named_scope("scatter_y"):
        sums = [
            moved(quarter(step).astype(jnp.bfloat16), pairs)
            for step, pairs in ((2, across), (1, up), (3, down))
        ]
        mine = quarter(0)
        for part in sums:
            mine = mine + part.astype(jnp.float32)
    with jax.named_scope("pair_z"):
        sent = mine.astype(jnp.bfloat16)
        back = moved(sent, other_half)
        aggregated = (sent.astype(jnp.float32) + back.astype(jnp.float32)).astype(jnp.bfloat16)
    with jax.named_scope("gather_y"):
        near = [aggregated] + [moved(aggregated, pairs) for pairs in (down, across, up)]
    with jax.named_scope("gather_core"):
        far = [moved(part, other_core) for part in near]
    out = finished(near, weight, bias)
    return finished(far, weight, bias, out)


def finish_kernel(mine, *refs):
    (parts, weight, bias), (out, stage, sems) = (refs[:4], *refs[4:6]), refs[-3:]
    y, core = lax.axis_index("y"), lax.axis_index("core")
    rows = parts[0].shape[0]
    half = core if mine else 1 - core
    copies = []
    for n in range(4):
        for m in range(0, rows, TILE):
            part = parts[n][m : m + TILE]
            result = jnp.dot(part, weight[...], preferred_element_type=jnp.float32) + bias[...]
            stage[n, m : m + TILE] = jnp.maximum(result, 0.0).astype(stage.dtype)
        quarter = (y + n) & 3
        start = pl.multiple_of((half * 4 + quarter) * rows, rows)
        copy = pltpu.make_async_copy(stage.at[n], out.at[pl.ds(start, rows)], sems.at[n])
        copy.start()
        copies.append(copy)
    for copy in copies:
        copy.wait()


def finished(parts, weight, bias, out=None):
    vmem, hbm = pl.BlockSpec(memory_space=pltpu.VMEM), pl.BlockSpec(memory_space=pl.ANY)
    rows = parts[0].shape[0]
    hidden = weight.shape[1]
    first = out is None
    return pl.pallas_call(
        functools.partial(finish_kernel, first),
        out_shape=jax.ShapeDtypeStruct((8 * rows, hidden), jnp.bfloat16),
        in_specs=[vmem] * 6 + ([] if first else [hbm]),
        out_specs=hbm,
        scratch_shapes=[
            pltpu.VMEM((4, rows, hidden), jnp.bfloat16),
            pltpu.SemaphoreType.DMA((4,)),
        ],
        input_output_aliases={} if first else {6: 0},
        cost_estimate=pl.CostEstimate(flops=150_000_000, bytes_accessed=2_000_000, transcendentals=0),
        compiler_params=pltpu.CompilerParams(vmem_limit_bytes=16 << 20),
        name="finish",
    )(*parts, weight, bias.reshape(1, hidden), *([] if first else [out]))


def solution(mesh):
    split = Mesh(mesh.devices.reshape(16, 2, 4, 2), AXES)
    rep = AXES[1:]
    in_specs = (
        P("blk", None),
        P(),
        P(),
        P("blk", rep, None, None, None),
        P("blk", rep, None),
        P("blk", rep),
    )
    return jax.shard_map(
        shards, mesh=split, in_specs=in_specs, out_specs=P("blk", None), check_vma=False
    )
```

```python
import functools

import jax
import jax.numpy as jnp
from jax import lax
from jax.experimental import pallas as pl
from jax.experimental.pallas import tpu as pltpu
from jax.sharding import Mesh
from jax.sharding import PartitionSpec as P

TILE = 128
ROW_TILES = 32
HALF_TILES = 16
SLOTS = 160
UNROLL = 8
AXES = ("blk", "zh", "y", "core")
LIST = 128
VMEM = pltpu.MemorySpace.VMEM

SOURCES = (
    (
        0x0262684ec3a14507, 0x12025a6e8fc3470d, 0x140074a8cf6325eb, 0x07245d98e3016bcf,
        0x00234271efc98bad, 0x0144502e67a9edcf, 0x1256470ea9ed8bcf, 0x00532c6a4b8defc9,
        0x20526170af43cbe9, 0x0742146583abcdef, 0x0524061783c9ebad, 0x023154e069abcf8d,
        0x0442b8c96105adef, 0x304a9c05216feb8d, 0x05cbc27e61af4d89, 0x0ecc83712fa96deb,
    ),
    (
        0x3135d4f109eb6527, 0x16337508e9a1254f, 0x174313ec09256b8f, 0x01413b7ec9256d8f,
        0x16250357c9a3ed8f, 0x3710536729cbaf8d, 0x173241870fcbade9, 0x0613459faf8bc9ed,
        0x165043578721c9ed, 0x3134520fc169eb8d, 0x01425635e1abcd8f, 0x7715326a0bc9ed8f,
        0x07215dff47a3cde9, 0x163eb8d74529adcf, 0x0389bf1427a9cfed, 0x09a8d53721cb4def,
    ),
)
PERMUTES = (
    (
        0x2200202001010101, 0x1220100001010101, 0x1202100001010101, 0x2100111001010101,
        0x0221001101010101, 0x2120100201010101, 0x1010010201010101, 0x2011020001010101,
        0x0212011001010101, 0x0120100101010101, 0x2100001101010101, 0x2011100001010101,
        0x2022100101010101, 0x1200100101010101, 0x2101201001010101, 0x2202011101010101,
    ),
    (
        0x0022010210101010, 0x2102021110101010, 0x2010021110101010, 0x1012000110101010,
        0x2112120010101010, 0x0201021010101010, 0x2201101010101010, 0x1100102210101010,
        0x2121100210101010, 0x2201011010101010, 0x1211210010101010, 0x0200011110101010,
        0x1210022010101010, 0x0121012010101010, 0x1012020110101010, 0x1011200010101010,
    ),
)


def digit(word, section):
    return word >> (4 * (15 - section)) & 15


def feature_routes():
    routes = ([], [], [])
    carriers = [0] * 512
    for chunk in range(2):
        for block in range(16):
            for section in range(16):
                replica = digit(SOURCES[chunk][block], section)
                carrier = digit(PERMUTES[chunk][block], section)
                assert chunk == (replica + carrier) % 2
                target = (block + section) % 16 * 16 + section
                routes[carrier].append((block * 16 + replica, target))
                carriers[2 * target + chunk] = carrier
    return routes, carriers


def device_pairs(step):
    pairs = []
    for index in range(256):
        blk, rest = divmod(index, 16)
        zh, rest = divmod(rest, 8)
        y, core = divmod(rest, 2)
        zh, y, core = step(zh, y, core)
        pairs.append((index, blk * 16 + zh * 8 + y * 2 + core))
    return pairs


def moved(value, pairs):
    return lax.ppermute(value, AXES, pairs)


def split_kernel(features, same, other, sems):
    rows = same.shape[0]
    core = lax.axis_index("core")
    copies = []
    for n, (start, piece) in enumerate(((core * rows, same), ((1 - core) * rows, other))):
        copy = pltpu.make_async_copy(features.at[pl.ds(start, rows)], piece, sems.at[n])
        copy.start()
        copies.append(copy)
    for copy in copies:
        copy.wait()


def pieces_of(features):
    piece = pltpu.VMEM((features.shape[0] // 2, features.shape[1]), features.dtype)
    return pl.pallas_call(
        split_kernel,
        out_shape=(piece, piece),
        in_specs=[pl.BlockSpec(memory_space=pltpu.HBM)],
        out_specs=(pl.BlockSpec(memory_space=pltpu.VMEM),) * 2,
        scratch_shapes=[pltpu.SemaphoreType.DMA((2,))],
        compiler_params=pltpu.CompilerParams(vmem_limit_bytes=1 << 20),
        name="split",
    )(pltpu.with_memory_space_constraint(features, pltpu.HBM))


def prepare_kernel(place, count, choice, tiles, held, zeros, slot_of, column_of, row_of, facts, position, sem):
    total = count[0]
    fetch = pltpu.make_async_copy(tiles, held, sem)
    fetch.start()
    zeros[...] = jnp.zeros_like(zeros)
    me = lax.axis_index(AXES)
    facts[1] = choice[2 * me]
    facts[2] = choice[2 * me + 1]

    for i in range(ROW_TILES + 1):
        position[i] = 0

    def number(k, carry):
        i = jnp.where(k < total, place[k] >> 5, ROW_TILES)
        position[i] = position[i] + 1
        return carry

    lax.fori_loop(0, SLOTS, number, 0, unroll=8)

    start = 0
    for i in range(ROW_TILES):
        n = position[i]
        position[i] = 2 * start
        start = start + ((n + 1) >> 1)
        last = jnp.where((n & 1) == 1, 2 * start - 1, 2 * LIST)
        slot_of[last] = 0
        column_of[last] = ROW_TILES
    facts[0] = start
    for u in range(UNROLL - 1):
        row_of[start + u] = 0
        for v in range(2):
            slot_of[2 * (start + u) + v] = 0
            column_of[2 * (start + u) + v] = ROW_TILES
    position[ROW_TILES] = 2 * LIST + 8

    def lay(k, carry):
        p = place[k]
        i = jnp.where(k < total, p >> 5, ROW_TILES)
        q = position[i]
        position[i] = q + jnp.where(k < total, 1, 0)
        slot_of[q] = k
        column_of[q] = p & (ROW_TILES - 1)
        row_of[q >> 1] = i & (ROW_TILES - 1)
        return carry

    lax.fori_loop(0, SLOTS, lay, 0, unroll=8)
    fetch.wait()


def prepared(tiles, place, count, choice):
    smem = pl.BlockSpec(memory_space=pltpu.SMEM)
    return pl.pallas_call(
        prepare_kernel,
        out_shape=(
            pltpu.VMEM((SLOTS, TILE, TILE), tiles.dtype),
            pltpu.VMEM((ROW_TILES, TILE, TILE), jnp.float32),
            jax.ShapeDtypeStruct((2 * LIST + 128,), jnp.int32),
            jax.ShapeDtypeStruct((2 * LIST + 128,), jnp.int32),
            jax.ShapeDtypeStruct((LIST + 128,), jnp.int32),
            jax.ShapeDtypeStruct((3,), jnp.int32),
        ),
        in_specs=[smem, smem, smem, pl.BlockSpec(memory_space=pltpu.HBM)],
        out_specs=(pl.BlockSpec(memory_space=pltpu.VMEM),) * 2 + (smem,) * 4,
        scratch_shapes=[
            pltpu.SMEM((ROW_TILES + 1,), jnp.int32),
            pltpu.SemaphoreType.DMA,
        ],
        cost_estimate=pl.CostEstimate(flops=0, bytes_accessed=16_000_000, transcendentals=0),
        compiler_params=pltpu.CompilerParams(vmem_limit_bytes=1 << 20),
        name="prepare",
    )(place, count, choice, pltpu.with_memory_space_constraint(tiles, pltpu.HBM))


def product_kernel(slot_of, column_of, row_of, facts, held, first, second, third, zeros, given, total, source):
    del zeros
    core = lax.axis_index("core")
    for chunk in range(2):
        for carrier, part in enumerate((first, second, third)):

            @pl.when(facts[1 + chunk] == carrier)
            def _():
                source[pl.ds(chunk * HALF_TILES, HALF_TILES)] = part[...]

    source[ROW_TILES] = jnp.zeros((TILE, TILE), source.dtype)

    steps = (facts[0] + UNROLL - 1) // UNROLL

    @pl.loop(0, steps)
    def _(step):
        start = step * UNROLL
        terms = []
        for u in range(UNROLL):
            q = 2 * (start + u)
            left = jnp.concatenate([held[slot_of[q]], held[slot_of[q + 1]]], axis=1)
            right = jnp.concatenate([source[column_of[q]], source[column_of[q + 1]]], axis=0)
            terms.append(jnp.dot(left, right, preferred_element_type=jnp.float32))
        for u in range(UNROLL):
            row = row_of[start + u]
            total[row] = total[row] + terms[u]

    given[...] = total[pl.ds((1 - core) * HALF_TILES, HALF_TILES)].astype(given.dtype)


def products(lists, held, zeros, parts):
    smem = pl.BlockSpec(memory_space=pltpu.SMEM)
    vmem = pl.BlockSpec(memory_space=pltpu.VMEM)
    tiles = [part.reshape(HALF_TILES, TILE, TILE) for part in parts]
    return pl.pallas_call(
        product_kernel,
        out_shape=(
            jax.ShapeDtypeStruct((HALF_TILES, TILE, TILE), jnp.bfloat16),
            jax.ShapeDtypeStruct((ROW_TILES, TILE, TILE), jnp.float32),
        ),
        in_specs=[smem] * 4 + [vmem] * 5,
        out_specs=(vmem, vmem),
        scratch_shapes=[pltpu.VMEM((ROW_TILES + 1, TILE, TILE), parts[0].dtype)],
        cost_estimate=pl.CostEstimate(flops=800_000_000, bytes_accessed=9_000_000, transcendentals=0),
        compiler_params=pltpu.CompilerParams(vmem_limit_bytes=8 << 20),
        input_output_aliases={8: 1},
        name="products",
    )(*lists, held, *tiles, zeros)


def shards(features, weight, bias, tile_values, tile_place, tile_count):
    y, core = lax.axis_index("y"), lax.axis_index("core")
    routes, carriers = feature_routes()
    same, other = pieces_of(features)
    parts = [moved(piece, route) for piece, route in zip((same, other, same), routes)]
    held, zeros, *lists = prepared(
        tile_values[0, 0], tile_place[0, 0], tile_count[0], jnp.asarray(carriers, jnp.int32)
    )

    other_core = device_pairs(lambda zh, y, core: (zh, y, 1 - core))
    other_half = device_pairs(lambda zh, y, core: (1 - zh, y, core))
    up = device_pairs(lambda zh, y, core: (zh, (y + 1) % 4, core))
    down = device_pairs(lambda zh, y, core: (zh, (y - 1) % 4, core))
    across = device_pairs(lambda zh, y, core: (zh, (y + 2) % 4, core))

    given, total = products(lists, held, zeros, parts)
    arrived = moved(given, other_core)

    def quarter(step):
        at = ((y + step) % 4) * 4
        size = 4
        part = lax.dynamic_slice_in_dim(total, core * HALF_TILES + at, size)
        part = part + lax.dynamic_slice_in_dim(arrived, at, size).astype(jnp.float32)
        return part.reshape(size * TILE, TILE)

    with jax.named_scope("scatter_y"):
        sums = [
            moved(quarter(step).astype(jnp.bfloat16), pairs)
            for step, pairs in ((2, across), (1, up), (3, down))
        ]
        mine = quarter(0)
        for part in sums:
            mine = mine + part.astype(jnp.float32)
    with jax.named_scope("pair_z"):
        sent = mine.astype(jnp.bfloat16)
        back = moved(sent, other_half)
        aggregated = (sent.astype(jnp.float32) + back.astype(jnp.float32)).astype(jnp.bfloat16)
    with jax.named_scope("gather_y"):
        near = [aggregated] + [moved(aggregated, pairs) for pairs in (down, across, up)]
    with jax.named_scope("gather_core"):
        far = [moved(part, other_core) for part in near]
    pieces = near + far
    out = finished(tuple(range(7)), pieces[:7], weight, bias)
    return finished((7,), pieces[7:], weight, bias, out)


def finish_kernel(places, *refs):
    (parts, weight, bias), (out, stage, sems) = (refs[: len(places)], *refs[len(places) :][:2]), refs[-3:]
    y, core = lax.axis_index("y"), lax.axis_index("core")
    rows = parts[0].shape[0]
    copies = []
    for n, place in enumerate(places):
        for m in range(0, rows, TILE):
            part = parts[n][m : m + TILE]
            result = jnp.dot(part, weight[...], preferred_element_type=jnp.float32) + bias[...]
            stage[n, m : m + TILE] = jnp.maximum(result, 0.0).astype(stage.dtype)
        half = core if place < 4 else 1 - core
        quarter = (y + place) & 3
        start = pl.multiple_of((half * 4 + quarter) * rows, rows)
        copy = pltpu.make_async_copy(stage.at[n], out.at[pl.ds(start, rows)], sems.at[n])
        copy.start()
        copies.append(copy)
    for copy in copies:
        copy.wait()


def finished(places, parts, weight, bias, out=None):
    vmem, hbm = pl.BlockSpec(memory_space=pltpu.VMEM), pl.BlockSpec(memory_space=pl.ANY)
    rows = parts[0].shape[0]
    hidden = weight.shape[1]
    number = len(places)
    first = out is None
    return pl.pallas_call(
        functools.partial(finish_kernel, places),
        out_shape=jax.ShapeDtypeStruct((8 * rows, hidden), jnp.bfloat16),
        in_specs=[vmem] * (number + 2) + ([] if first else [hbm]),
        out_specs=hbm,
        scratch_shapes=[
            pltpu.VMEM((number, rows, hidden), jnp.bfloat16),
            pltpu.SemaphoreType.DMA((number,)),
        ],
        input_output_aliases={} if first else {number + 2: 0},
        cost_estimate=pl.CostEstimate(
            flops=40_000_000 * number, bytes_accessed=500_000 * number, transcendentals=0
        ),
        compiler_params=pltpu.CompilerParams(vmem_limit_bytes=16 << 20),
        name="finish",
    )(*parts, weight, bias.reshape(1, hidden), *([] if first else [out]))


def solution(mesh):
    split = Mesh(mesh.devices.reshape(16, 2, 4, 2), AXES)
    rep = AXES[1:]
    in_specs = (
        P("blk", None),
        P(),
        P(),
        P("blk", rep, None, None, None),
        P("blk", rep, None),
        P("blk", rep),
    )
    return jax.shard_map(
        shards, mesh=split, in_specs=in_specs, out_specs=P("blk", None), check_vma=False
    )
```

```python
import functools

import jax
import jax.numpy as jnp
from jax import lax
from jax.experimental import pallas as pl
from jax.experimental.pallas import tpu as pltpu
from jax.sharding import Mesh
from jax.sharding import PartitionSpec as P

TILE = 128
ROW_TILES = 32
HALF_TILES = 16
SLOTS = 160
UNROLL = 8
AXES = ("blk", "zh", "y", "core")
LIST = 128
VMEM = pltpu.MemorySpace.VMEM

SOURCES = (
    (
        0x0262684ec3a14507, 0x12025a6e8fc3470d, 0x140074a8cf6325eb, 0x07245d98e3016bcf,
        0x00234271efc98bad, 0x0144502e67a9edcf, 0x1256470ea9ed8bcf, 0x00532c6a4b8defc9,
        0x20526170af43cbe9, 0x0742146583abcdef, 0x0524061783c9ebad, 0x023154e069abcf8d,
        0x0442b8c96105adef, 0x304a9c05216feb8d, 0x05cbc27e61af4d89, 0x0ecc83712fa96deb,
    ),
    (
        0x3135d4f109eb6527, 0x16337508e9a1254f, 0x174313ec09256b8f, 0x01413b7ec9256d8f,
        0x16250357c9a3ed8f, 0x3710536729cbaf8d, 0x173241870fcbade9, 0x0613459faf8bc9ed,
        0x165043578721c9ed, 0x3134520fc169eb8d, 0x01425635e1abcd8f, 0x7715326a0bc9ed8f,
        0x07215dff47a3cde9, 0x163eb8d74529adcf, 0x0389bf1427a9cfed, 0x09a8d53721cb4def,
    ),
)
PERMUTES = (
    (
        0x2200202001010101, 0x1220100001010101, 0x1202100001010101, 0x2100111001010101,
        0x0221001101010101, 0x2120100201010101, 0x1010010201010101, 0x2011020001010101,
        0x0212011001010101, 0x0120100101010101, 0x2100001101010101, 0x2011100001010101,
        0x2022100101010101, 0x1200100101010101, 0x2101201001010101, 0x2202011101010101,
    ),
    (
        0x0022010210101010, 0x2102021110101010, 0x2010021110101010, 0x1012000110101010,
        0x2112120010101010, 0x0201021010101010, 0x2201101010101010, 0x1100102210101010,
        0x2121100210101010, 0x2201011010101010, 0x1211210010101010, 0x0200011110101010,
        0x1210022010101010, 0x0121012010101010, 0x1012020110101010, 0x1011200010101010,
    ),
)


def digit(word, section):
    return word >> (4 * (15 - section)) & 15


def feature_routes():
    routes = ([], [], [])
    carriers = [0] * 512
    for chunk in range(2):
        for block in range(16):
            for section in range(16):
                replica = digit(SOURCES[chunk][block], section)
                carrier = digit(PERMUTES[chunk][block], section)
                assert chunk == (replica + carrier) % 2
                target = (block + section) % 16 * 16 + section
                routes[carrier].append((block * 16 + replica, target))
                carriers[2 * target + chunk] = carrier
    return routes, carriers


def device_pairs(step):
    pairs = []
    for index in range(256):
        blk, rest = divmod(index, 16)
        zh, rest = divmod(rest, 8)
        y, core = divmod(rest, 2)
        zh, y, core = step(zh, y, core)
        pairs.append((index, blk * 16 + zh * 8 + y * 2 + core))
    return pairs


def moved(value, pairs):
    return lax.ppermute(value, AXES, pairs)


def split_kernel(features, same, other, sems):
    rows = same.shape[0]
    core = lax.axis_index("core")
    copies = []
    for n, (start, piece) in enumerate(((core * rows, same), ((1 - core) * rows, other))):
        copy = pltpu.make_async_copy(features.at[pl.ds(start, rows)], piece, sems.at[n])
        copy.start()
        copies.append(copy)
    for copy in copies:
        copy.wait()


def pieces_of(features):
    piece = pltpu.VMEM((features.shape[0] // 2, features.shape[1]), features.dtype)
    return pl.pallas_call(
        split_kernel,
        out_shape=(piece, piece),
        in_specs=[pl.BlockSpec(memory_space=pltpu.HBM)],
        out_specs=(pl.BlockSpec(memory_space=pltpu.VMEM),) * 2,
        scratch_shapes=[pltpu.SemaphoreType.DMA((2,))],
        compiler_params=pltpu.CompilerParams(vmem_limit_bytes=1 << 20),
        name="split",
    )(pltpu.with_memory_space_constraint(features, pltpu.HBM))


def prepare_kernel(place, count, choice, tiles, held, zeros, slot_of, column_of, row_of, facts, position, sem):
    total = count[0]
    fetch = pltpu.make_async_copy(tiles, held, sem)
    fetch.start()
    zeros[...] = jnp.zeros_like(zeros)
    me = lax.axis_index(AXES)
    facts[1] = choice[2 * me]
    facts[2] = choice[2 * me + 1]

    for i in range(ROW_TILES + 1):
        position[i] = 0

    def number(k, carry):
        i = jnp.where(k < total, place[k] >> 5, ROW_TILES)
        position[i] = position[i] + 1
        return carry

    lax.fori_loop(0, SLOTS, number, 0, unroll=8)

    start = 0
    for i in range(ROW_TILES):
        n = position[i]
        position[i] = 2 * start
        start = start + ((n + 1) >> 1)
        last = jnp.where((n & 1) == 1, 2 * start - 1, 2 * LIST)
        slot_of[last] = 0
        column_of[last] = ROW_TILES
    facts[0] = start
    for u in range(UNROLL - 1):
        row_of[start + u] = 0
        for v in range(2):
            slot_of[2 * (start + u) + v] = 0
            column_of[2 * (start + u) + v] = ROW_TILES
    position[ROW_TILES] = 2 * LIST + 8

    def lay(k, carry):
        p = place[k]
        i = jnp.where(k < total, p >> 5, ROW_TILES)
        q = position[i]
        position[i] = q + jnp.where(k < total, 1, 0)
        slot_of[q] = k
        column_of[q] = p & (ROW_TILES - 1)
        row_of[q >> 1] = i & (ROW_TILES - 1)
        return carry

    lax.fori_loop(0, SLOTS, lay, 0, unroll=8)
    fetch.wait()


def prepared(tiles, place, count, choice):
    smem = pl.BlockSpec(memory_space=pltpu.SMEM)
    return pl.pallas_call(
        prepare_kernel,
        out_shape=(
            pltpu.VMEM((SLOTS, TILE, TILE), tiles.dtype),
            pltpu.VMEM((ROW_TILES, TILE, TILE), jnp.float32),
            jax.ShapeDtypeStruct((2 * LIST + 128,), jnp.int32),
            jax.ShapeDtypeStruct((2 * LIST + 128,), jnp.int32),
            jax.ShapeDtypeStruct((LIST + 128,), jnp.int32),
            jax.ShapeDtypeStruct((3,), jnp.int32),
        ),
        in_specs=[smem, smem, smem, pl.BlockSpec(memory_space=pltpu.HBM)],
        out_specs=(pl.BlockSpec(memory_space=pltpu.VMEM),) * 2 + (smem,) * 4,
        scratch_shapes=[
            pltpu.SMEM((ROW_TILES + 1,), jnp.int32),
            pltpu.SemaphoreType.DMA,
        ],
        cost_estimate=pl.CostEstimate(flops=0, bytes_accessed=16_000_000, transcendentals=0),
        compiler_params=pltpu.CompilerParams(vmem_limit_bytes=1 << 20),
        name="prepare",
    )(place, count, choice, pltpu.with_memory_space_constraint(tiles, pltpu.HBM))


def product_kernel(slot_of, column_of, row_of, facts, held, first, second, third, zeros, given, total, source):
    del zeros
    core = lax.axis_index("core")
    for chunk in range(2):
        for carrier, part in enumerate((first, second, third)):

            @pl.when(facts[1 + chunk] == carrier)
            def _():
                source[pl.ds(chunk * HALF_TILES, HALF_TILES)] = part[...]

    source[ROW_TILES] = jnp.zeros((TILE, TILE), source.dtype)

    steps = (facts[0] + UNROLL - 1) // UNROLL

    @pl.loop(0, steps)
    def _(step):
        start = step * UNROLL
        terms = []
        for u in range(UNROLL):
            q = 2 * (start + u)
            left = jnp.concatenate([held[slot_of[q]], held[slot_of[q + 1]]], axis=1)
            right = jnp.concatenate([source[column_of[q]], source[column_of[q + 1]]], axis=0)
            terms.append(jnp.dot(left, right, preferred_element_type=jnp.float32))
        for u in range(UNROLL):
            row = row_of[start + u]
            total[row] = total[row] + terms[u]

    given[...] = total[pl.ds((1 - core) * HALF_TILES, HALF_TILES)].astype(given.dtype)


def products(lists, held, zeros, parts):
    smem = pl.BlockSpec(memory_space=pltpu.SMEM)
    vmem = pl.BlockSpec(memory_space=pltpu.VMEM)
    tiles = [part.reshape(HALF_TILES, TILE, TILE) for part in parts]
    return pl.pallas_call(
        product_kernel,
        out_shape=(
            jax.ShapeDtypeStruct((HALF_TILES, TILE, TILE), jnp.bfloat16),
            jax.ShapeDtypeStruct((ROW_TILES, TILE, TILE), jnp.float32),
        ),
        in_specs=[smem] * 4 + [vmem] * 5,
        out_specs=(vmem, vmem),
        scratch_shapes=[pltpu.VMEM((ROW_TILES + 1, TILE, TILE), parts[0].dtype)],
        cost_estimate=pl.CostEstimate(flops=800_000_000, bytes_accessed=9_000_000, transcendentals=0),
        compiler_params=pltpu.CompilerParams(vmem_limit_bytes=8 << 20),
        input_output_aliases={8: 1},
        name="products",
    )(*lists, held, *tiles, zeros)


def shards(features, weight, bias, tile_values, tile_place, tile_count):
    y, core = lax.axis_index("y"), lax.axis_index("core")
    routes, carriers = feature_routes()
    same, other = pieces_of(features)
    parts = [moved(piece, route) for piece, route in zip((same, other, same), routes)]
    held, zeros, *lists = prepared(
        tile_values[0, 0], tile_place[0, 0], tile_count[0], jnp.asarray(carriers, jnp.int32)
    )

    other_core = device_pairs(lambda zh, y, core: (zh, y, 1 - core))
    other_half = device_pairs(lambda zh, y, core: (1 - zh, y, core))
    up = device_pairs(lambda zh, y, core: (zh, (y + 1) % 4, core))
    down = device_pairs(lambda zh, y, core: (zh, (y - 1) % 4, core))
    across = device_pairs(lambda zh, y, core: (zh, (y + 2) % 4, core))

    given, total = products(lists, held, zeros, parts)
    arrived = moved(given, other_core)

    def quarter(step):
        at = ((y + step) % 4) * 4
        size = 4
        part = lax.dynamic_slice_in_dim(total, core * HALF_TILES + at, size)
        part = part + lax.dynamic_slice_in_dim(arrived, at, size).astype(jnp.float32)
        return part.reshape(size * TILE, TILE)

    with jax.named_scope("scatter_y"):
        sums = [
            moved(quarter(step).astype(jnp.bfloat16), pairs)
            for step, pairs in ((2, across), (1, up), (3, down))
        ]
        mine = quarter(0)
        for part in sums:
            mine = mine + part.astype(jnp.float32)
    with jax.named_scope("pair_z"):
        sent = mine.astype(jnp.bfloat16)
        back = moved(sent, other_half)
        aggregated = (sent.astype(jnp.float32) + back.astype(jnp.float32)).astype(jnp.bfloat16)
    with jax.named_scope("gather_y"):
        near = [aggregated] + [moved(aggregated, pairs) for pairs in (down, across, up)]
    with jax.named_scope("gather_core"):
        far = [moved(part, other_core) for part in near]
    pieces = near + far
    out = finished(tuple(range(4)), pieces[:4], weight, bias)
    return finished(tuple(range(4, 8)), pieces[4:], weight, bias, out)


def finish_kernel(places, *refs):
    (parts, weight, bias), (out, stage, sems) = (refs[: len(places)], *refs[len(places) :][:2]), refs[-3:]
    y, core = lax.axis_index("y"), lax.axis_index("core")
    rows = parts[0].shape[0]
    copies = []
    for n, place in enumerate(places):
        for m in range(0, rows, TILE):
            part = parts[n][m : m + TILE]
            result = jnp.dot(part, weight[...], preferred_element_type=jnp.float32) + bias[...]
            stage[n, m : m + TILE] = jnp.maximum(result, 0.0).astype(stage.dtype)
        half = core if place < 4 else 1 - core
        quarter = (y + place) & 3
        start = pl.multiple_of((half * 4 + quarter) * rows, rows)
        copy = pltpu.make_async_copy(stage.at[n], out.at[pl.ds(start, rows)], sems.at[n])
        copy.start()
        copies.append(copy)
    for copy in copies:
        copy.wait()


def finished(places, parts, weight, bias, out=None):
    vmem, hbm = pl.BlockSpec(memory_space=pltpu.VMEM), pl.BlockSpec(memory_space=pl.ANY)
    rows = parts[0].shape[0]
    hidden = weight.shape[1]
    number = len(places)
    first = out is None
    return pl.pallas_call(
        functools.partial(finish_kernel, places),
        out_shape=jax.ShapeDtypeStruct((8 * rows, hidden), jnp.bfloat16),
        in_specs=[vmem] * (number + 2) + ([] if first else [hbm]),
        out_specs=hbm,
        scratch_shapes=[
            pltpu.VMEM((number, rows, hidden), jnp.bfloat16),
            pltpu.SemaphoreType.DMA((number,)),
        ],
        input_output_aliases={} if first else {number + 2: 0},
        cost_estimate=pl.CostEstimate(
            flops=40_000_000 * number, bytes_accessed=500_000 * number, transcendentals=0
        ),
        compiler_params=pltpu.CompilerParams(vmem_limit_bytes=16 << 20),
        name="finish",
    )(*parts, weight, bias.reshape(1, hidden), *([] if first else [out]))


def solution(mesh):
    split = Mesh(mesh.devices.reshape(16, 2, 4, 2), AXES)
    rep = AXES[1:]
    in_specs = (
        P("blk", None),
        P(),
        P(),
        P("blk", rep, None, None, None),
        P("blk", rep, None),
        P("blk", rep),
    )
    return jax.shard_map(
        shards, mesh=split, in_specs=in_specs, out_specs=P("blk", None), check_vma=False
    )
```

```python
import functools

import jax
import jax.numpy as jnp
from jax import lax
from jax.experimental import pallas as pl
from jax.experimental.pallas import tpu as pltpu
from jax.sharding import Mesh
from jax.sharding import PartitionSpec as P

TILE = 128
ROW_TILES = 32
HALF_TILES = 16
SLOTS = 160
UNROLL = 8
AXES = ("blk", "zh", "y", "core")
LIST = 128
VMEM = pltpu.MemorySpace.VMEM

SOURCES = (
    (
        0x0262684ec3a14507, 0x12025a6e8fc3470d, 0x140074a8cf6325eb, 0x07245d98e3016bcf,
        0x00234271efc98bad, 0x0144502e67a9edcf, 0x1256470ea9ed8bcf, 0x00532c6a4b8defc9,
        0x20526170af43cbe9, 0x0742146583abcdef, 0x0524061783c9ebad, 0x023154e069abcf8d,
        0x0442b8c96105adef, 0x304a9c05216feb8d, 0x05cbc27e61af4d89, 0x0ecc83712fa96deb,
    ),
    (
        0x3135d4f109eb6527, 0x16337508e9a1254f, 0x174313ec09256b8f, 0x01413b7ec9256d8f,
        0x16250357c9a3ed8f, 0x3710536729cbaf8d, 0x173241870fcbade9, 0x0613459faf8bc9ed,
        0x165043578721c9ed, 0x3134520fc169eb8d, 0x01425635e1abcd8f, 0x7715326a0bc9ed8f,
        0x07215dff47a3cde9, 0x163eb8d74529adcf, 0x0389bf1427a9cfed, 0x09a8d53721cb4def,
    ),
)
PERMUTES = (
    (
        0x2200202001010101, 0x1220100001010101, 0x1202100001010101, 0x2100111001010101,
        0x0221001101010101, 0x2120100201010101, 0x1010010201010101, 0x2011020001010101,
        0x0212011001010101, 0x0120100101010101, 0x2100001101010101, 0x2011100001010101,
        0x2022100101010101, 0x1200100101010101, 0x2101201001010101, 0x2202011101010101,
    ),
    (
        0x0022010210101010, 0x2102021110101010, 0x2010021110101010, 0x1012000110101010,
        0x2112120010101010, 0x0201021010101010, 0x2201101010101010, 0x1100102210101010,
        0x2121100210101010, 0x2201011010101010, 0x1211210010101010, 0x0200011110101010,
        0x1210022010101010, 0x0121012010101010, 0x1012020110101010, 0x1011200010101010,
    ),
)


def digit(word, section):
    return word >> (4 * (15 - section)) & 15


def feature_routes():
    routes = ([], [], [])
    carriers = [0] * 512
    for chunk in range(2):
        for block in range(16):
            for section in range(16):
                replica = digit(SOURCES[chunk][block], section)
                carrier = digit(PERMUTES[chunk][block], section)
                assert chunk == (replica + carrier) % 2
                target = (block + section) % 16 * 16 + section
                routes[carrier].append((block * 16 + replica, target))
                carriers[2 * target + chunk] = carrier
    return routes, carriers


def device_pairs(step):
    pairs = []
    for index in range(256):
        blk, rest = divmod(index, 16)
        zh, rest = divmod(rest, 8)
        y, core = divmod(rest, 2)
        zh, y, core = step(zh, y, core)
        pairs.append((index, blk * 16 + zh * 8 + y * 2 + core))
    return pairs


def moved(value, pairs):
    return lax.ppermute(value, AXES, pairs)


def split_kernel(features, same, other, sems):
    rows = same.shape[0]
    core = lax.axis_index("core")
    copies = []
    for n, (start, piece) in enumerate(((core * rows, same), ((1 - core) * rows, other))):
        copy = pltpu.make_async_copy(features.at[pl.ds(start, rows)], piece, sems.at[n])
        copy.start()
        copies.append(copy)
    for copy in copies:
        copy.wait()


def pieces_of(features):
    piece = pltpu.VMEM((features.shape[0] // 2, features.shape[1]), features.dtype)
    return pl.pallas_call(
        split_kernel,
        out_shape=(piece, piece),
        in_specs=[pl.BlockSpec(memory_space=pltpu.HBM)],
        out_specs=(pl.BlockSpec(memory_space=pltpu.VMEM),) * 2,
        scratch_shapes=[pltpu.SemaphoreType.DMA((2,))],
        compiler_params=pltpu.CompilerParams(vmem_limit_bytes=1 << 20),
        name="split",
    )(pltpu.with_memory_space_constraint(features, pltpu.HBM))


def prepare_kernel(place, count, choice, tiles, held, zeros, slot_of, column_of, row_of, facts, position, sem):
    total = count[0]
    fetch = pltpu.make_async_copy(tiles, held, sem)
    fetch.start()
    zeros[...] = jnp.zeros_like(zeros)
    me = lax.axis_index(AXES)
    facts[1] = choice[2 * me]
    facts[2] = choice[2 * me + 1]

    for i in range(ROW_TILES + 1):
        position[i] = 0

    def number(k, carry):
        i = jnp.where(k < total, place[k] >> 5, ROW_TILES)
        position[i] = position[i] + 1
        return carry

    lax.fori_loop(0, SLOTS, number, 0, unroll=8)

    start = 0
    for i in range(ROW_TILES):
        n = position[i]
        position[i] = 2 * start
        start = start + ((n + 1) >> 1)
        last = jnp.where((n & 1) == 1, 2 * start - 1, 2 * LIST)
        slot_of[last] = 0
        column_of[last] = ROW_TILES
    facts[0] = start
    for u in range(UNROLL - 1):
        row_of[start + u] = 0
        for v in range(2):
            slot_of[2 * (start + u) + v] = 0
            column_of[2 * (start + u) + v] = ROW_TILES
    position[ROW_TILES] = 2 * LIST + 8

    def lay(k, carry):
        p = place[k]
        i = jnp.where(k < total, p >> 5, ROW_TILES)
        q = position[i]
        position[i] = q + jnp.where(k < total, 1, 0)
        slot_of[q] = k
        column_of[q] = p & (ROW_TILES - 1)
        row_of[q >> 1] = i & (ROW_TILES - 1)
        return carry

    lax.fori_loop(0, SLOTS, lay, 0, unroll=8)
    fetch.wait()


def prepared(tiles, place, count, choice):
    smem = pl.BlockSpec(memory_space=pltpu.SMEM)
    return pl.pallas_call(
        prepare_kernel,
        out_shape=(
            pltpu.VMEM((SLOTS, TILE, TILE), tiles.dtype),
            pltpu.VMEM((ROW_TILES, TILE, TILE), jnp.float32),
            jax.ShapeDtypeStruct((2 * LIST + 128,), jnp.int32),
            jax.ShapeDtypeStruct((2 * LIST + 128,), jnp.int32),
            jax.ShapeDtypeStruct((LIST + 128,), jnp.int32),
            jax.ShapeDtypeStruct((3,), jnp.int32),
        ),
        in_specs=[smem, smem, smem, pl.BlockSpec(memory_space=pltpu.HBM)],
        out_specs=(pl.BlockSpec(memory_space=pltpu.VMEM),) * 2 + (smem,) * 4,
        scratch_shapes=[
            pltpu.SMEM((ROW_TILES + 1,), jnp.int32),
            pltpu.SemaphoreType.DMA,
        ],
        cost_estimate=pl.CostEstimate(flops=0, bytes_accessed=16_000_000, transcendentals=0),
        compiler_params=pltpu.CompilerParams(vmem_limit_bytes=1 << 20),
        name="prepare",
    )(place, count, choice, pltpu.with_memory_space_constraint(tiles, pltpu.HBM))


def product_kernel(slot_of, column_of, row_of, facts, held, first, second, third, zeros, given, total, source):
    del zeros
    core = lax.axis_index("core")
    for chunk in range(2):
        for carrier, part in enumerate((first, second, third)):

            @pl.when(facts[1 + chunk] == carrier)
            def _():
                source[pl.ds(chunk * HALF_TILES, HALF_TILES)] = part[...]

    source[ROW_TILES] = jnp.zeros((TILE, TILE), source.dtype)

    steps = (facts[0] + UNROLL - 1) // UNROLL

    @pl.loop(0, steps)
    def _(step):
        start = step * UNROLL
        terms = []
        for u in range(UNROLL):
            q = 2 * (start + u)
            left = jnp.concatenate([held[slot_of[q]], held[slot_of[q + 1]]], axis=1)
            right = jnp.concatenate([source[column_of[q]], source[column_of[q + 1]]], axis=0)
            terms.append(jnp.dot(left, right, preferred_element_type=jnp.float32))
        for u in range(UNROLL):
            row = row_of[start + u]
            total[row] = total[row] + terms[u]

    given[...] = total[pl.ds((1 - core) * HALF_TILES, HALF_TILES)].astype(given.dtype)


def products(lists, held, zeros, parts):
    smem = pl.BlockSpec(memory_space=pltpu.SMEM)
    vmem = pl.BlockSpec(memory_space=pltpu.VMEM)
    tiles = [part.reshape(HALF_TILES, TILE, TILE) for part in parts]
    return pl.pallas_call(
        product_kernel,
        out_shape=(
            jax.ShapeDtypeStruct((HALF_TILES, TILE, TILE), jnp.bfloat16),
            jax.ShapeDtypeStruct((ROW_TILES, TILE, TILE), jnp.float32),
        ),
        in_specs=[smem] * 4 + [vmem] * 5,
        out_specs=(vmem, vmem),
        scratch_shapes=[pltpu.VMEM((ROW_TILES + 1, TILE, TILE), parts[0].dtype)],
        cost_estimate=pl.CostEstimate(flops=800_000_000, bytes_accessed=9_000_000, transcendentals=0),
        compiler_params=pltpu.CompilerParams(vmem_limit_bytes=8 << 20),
        input_output_aliases={8: 1},
        name="products",
    )(*lists, held, *tiles, zeros)


def shards(features, weight, bias, tile_values, tile_place, tile_count):
    y, core = lax.axis_index("y"), lax.axis_index("core")
    routes, carriers = feature_routes()
    same, other = pieces_of(features)
    parts = [moved(piece, route) for piece, route in zip((same, other, same), routes)]
    held, zeros, *lists = prepared(
        tile_values[0, 0], tile_place[0, 0], tile_count[0], jnp.asarray(carriers, jnp.int32)
    )

    other_core = device_pairs(lambda zh, y, core: (zh, y, 1 - core))
    other_half = device_pairs(lambda zh, y, core: (1 - zh, y, core))
    up = device_pairs(lambda zh, y, core: (zh, (y + 1) % 4, core))
    down = device_pairs(lambda zh, y, core: (zh, (y - 1) % 4, core))
    across = device_pairs(lambda zh, y, core: (zh, (y + 2) % 4, core))

    given, total = products(lists, held, zeros, parts)
    arrived = moved(given, other_core)

    def quarter(step):
        at = ((y + step) % 4) * 4
        size = 4
        part = lax.dynamic_slice_in_dim(total, core * HALF_TILES + at, size)
        part = part + lax.dynamic_slice_in_dim(arrived, at, size).astype(jnp.float32)
        return part.reshape(size * TILE, TILE)

    with jax.named_scope("scatter_y"):
        sums = [
            moved(quarter(step).astype(jnp.bfloat16), pairs)
            for step, pairs in ((2, across), (1, up), (3, down))
        ]
        mine = quarter(0)
        for part in sums:
            mine = mine + part.astype(jnp.float32)
    with jax.named_scope("pair_z"):
        sent = mine.astype(jnp.bfloat16)
        back = moved(sent, other_half)
        aggregated = (sent.astype(jnp.float32) + back.astype(jnp.float32)).astype(jnp.bfloat16)
    with jax.named_scope("gather_y"):
        near = [aggregated] + [moved(aggregated, pairs) for pairs in (down, up, across)]
    with jax.named_scope("gather_core"):
        far = [moved(part, other_core) for part in near]
    pieces = near + far
    out = finished((0, 1, 3, 2), pieces[:4], weight, bias)
    return finished((4, 5, 7, 6), pieces[4:], weight, bias, out)


def finish_kernel(places, *refs):
    (parts, weight, bias), (out, stage, sems) = (refs[: len(places)], *refs[len(places) :][:2]), refs[-3:]
    y, core = lax.axis_index("y"), lax.axis_index("core")
    rows = parts[0].shape[0]
    copies = []
    for n, place in enumerate(places):
        for m in range(0, rows, TILE):
            part = parts[n][m : m + TILE]
            result = jnp.dot(part, weight[...], preferred_element_type=jnp.float32) + bias[...]
            stage[n, m : m + TILE] = jnp.maximum(result, 0.0).astype(stage.dtype)
        half = core if place < 4 else 1 - core
        quarter = (y + place) & 3
        start = pl.multiple_of((half * 4 + quarter) * rows, rows)
        copy = pltpu.make_async_copy(stage.at[n], out.at[pl.ds(start, rows)], sems.at[n])
        copy.start()
        copies.append(copy)
    for copy in copies:
        copy.wait()


def finished(places, parts, weight, bias, out=None):
    vmem, hbm = pl.BlockSpec(memory_space=pltpu.VMEM), pl.BlockSpec(memory_space=pl.ANY)
    rows = parts[0].shape[0]
    hidden = weight.shape[1]
    number = len(places)
    first = out is None
    return pl.pallas_call(
        functools.partial(finish_kernel, places),
        out_shape=jax.ShapeDtypeStruct((8 * rows, hidden), jnp.bfloat16),
        in_specs=[vmem] * (number + 2) + ([] if first else [hbm]),
        out_specs=hbm,
        scratch_shapes=[
            pltpu.VMEM((number, rows, hidden), jnp.bfloat16),
            pltpu.SemaphoreType.DMA((number,)),
        ],
        input_output_aliases={} if first else {number + 2: 0},
        cost_estimate=pl.CostEstimate(
            flops=40_000_000 * number, bytes_accessed=500_000 * number, transcendentals=0
        ),
        compiler_params=pltpu.CompilerParams(vmem_limit_bytes=16 << 20),
        name="finish",
    )(*parts, weight, bias.reshape(1, hidden), *([] if first else [out]))


def solution(mesh):
    split = Mesh(mesh.devices.reshape(16, 2, 4, 2), AXES)
    rep = AXES[1:]
    in_specs = (
        P("blk", None),
        P(),
        P(),
        P("blk", rep, None, None, None),
        P("blk", rep, None),
        P("blk", rep),
    )
    return jax.shard_map(
        shards, mesh=split, in_specs=in_specs, out_specs=P("blk", None), check_vma=False
    )
```
